32 devices in a mesh: row: 4 (over z), col: 4 (over y, x), leaf: 2 (over core).
Axes of the slice: x: 2, y: 2, z: 4, core: 2. Of those that a mesh axis runs over, the one named last changes fastest.
Arguments:
- separator: float32 [8192, 16384], P('row', 'col'), may hold values from -6 to 6
- col_panels: bfloat16 [2, 8192, 1536], P('leaf', 'row', 'col'), may hold values from -0.15625 to 0.15625
- row_panels: bfloat16 [2, 1536, 16384], P('leaf', 'row', 'col'), may hold values from -6 to 6
- rows_list: int32 [2, 6, 16], replicated, may hold values from 0 to 63
- cols_list: int32 [2, 6, 32], replicated, may hold values from 0 to 127
- inverses: float32 [8192, 256], P('row'), may hold values from -0.375 to 0.375
Outputs:
- solved: float32 [8192, 16384], P('row', ('col', 'leaf'))
The draws below stay inside these ranges and needn't reach their ends.
All inputs are finite; a program needn't handle non-finite values.
Results may differ from the reference program's by a relative error of at most 0.0003.
Values may be sent and summed in bfloat16 or wider, within the bound.
A program may use at most 192 MiB of HBM per device.

```python
import jax
import jax.numpy as jnp
from jax import lax

NS = 8192
W = 256
K = 6
BLK = 128
RB = 16
CB = 32
NCOLS = 16384
KW = 1536


def with_ends(drawn, rng, least, top_value):
    spot = [jax.random.randint(jax.random.fold_in(rng, axis), (), 0, length) for axis, length in enumerate(drawn.shape)]
    longest = drawn.shape.index(max(drawn.shape))
    neighbour = spot[:longest] + [(spot[longest] + 1) % drawn.shape[longest]] + spot[longest + 1:]
    return drawn.at[tuple(spot)].set(least).at[tuple(neighbour)].set(top_value)


def levels(key, extent, split, low, largest):
    gain = 1.0
    for axis_at, blocks in split:
        steps = jax.random.uniform(jax.random.fold_in(jax.random.fold_in(key, 6), axis_at), (blocks,), jnp.float32, low / len(split), largest / len(split))
        gain = gain * jnp.repeat(jnp.exp(steps), extent[axis_at] // blocks).reshape((-1,) + (1,) * (len(extent) - 1 - axis_at))
    return gain


def normal_values(rng, extent, spread, limit, pieces=(), held_as=jnp.bfloat16):
    array = jax.random.normal(rng, extent, jnp.float32) * spread
    if len(pieces) > 0:
        array = levels(rng, extent, pieces, -0.22, 0.18) * array
    return jnp.clip(array, min=-limit, max=limit).astype(held_as)


def setup_inputs(seed: int = 0) -> dict:
    key_list = jax.random.split(jax.random.key(seed), 7)
    separator = normal_values(key_list[0], (NS, NCOLS), 1.0, 6.0, ((0, 4), (1, 4)), jnp.float32)
    col_panels = normal_values(key_list[1], (2, NS, KW), KW ** -0.5, 0.15625, ((0, 2), (1, 4), (2, 4)))
    row_panels = normal_values(key_list[2], (2, KW, NCOLS), 1.0, 6.0, ((0, 2), (1, 4), (2, 4)))
    rows_list = with_ends(jax.random.randint(key_list[3], (2, K, RB), 0, NS // BLK), jax.random.fold_in(key_list[3], 1), 0, (NS // BLK) - 1).astype(jnp.int32)
    cols_list = with_ends(jax.random.randint(key_list[4], (2, K, CB), 0, NCOLS // BLK), jax.random.fold_in(key_list[4], 1), 0, (NCOLS // BLK) - 1).astype(jnp.int32)
    inverses = normal_values(key_list[5], (NS, W), W ** -0.5, 0.375, ((0, 4),), jnp.float32)
    return {"separator": separator, "col_panels": col_panels, "row_panels": row_panels, "rows_list": rows_list, "cols_list": cols_list, "inverses": inverses}


def subtree_update(lower_raw, upper_raw, row_list, col_list):
    row_block = jnp.arange(NS, dtype=jnp.int32) // BLK
    col_block = jnp.arange(NCOLS, dtype=jnp.int32) // BLK
    row_mask = jnp.any(row_list[:, :, None] == row_block[None, None, :], axis=1)
    col_mask = jnp.any(col_list[:, :, None] == col_block[None, None, :], axis=1)
    owner = jnp.arange(KW, dtype=jnp.int32) // W
    lower = jnp.where(row_mask[owner].T, lower_raw, jnp.zeros_like(lower_raw))
    upper = jnp.where(col_mask[owner], upper_raw, jnp.zeros_like(upper_raw))
    return jnp.dot(lower, upper, preferred_element_type=jnp.float32)


def reference(separator, col_panels, row_panels, rows_list, cols_list, inverses):
    combined = separator - subtree_update(col_panels[0], row_panels[0], rows_list[0], cols_list[0])
    combined = combined - subtree_update(col_panels[1], row_panels[1], rows_list[1], cols_list[1])
    blocks = combined.reshape(NS // W, W, NCOLS)
    factor = inverses.reshape(NS // W, W, W)
    solved = jnp.einsum("bij,bjc->bic", factor, blocks, precision=lax.Precision.HIGHEST)
    return solved.reshape(NS, NCOLS)
```

```python
import functools

import jax
import jax.numpy as jnp
from jax import lax
from jax.experimental import pallas as pl
from jax.experimental.pallas import tpu as pltpu
from jax.sharding import PartitionSpec as P

W = 256
BLK = 128
MESH = pl.DeviceIdType.MESH
PARTS = 2
LEAFROWS = 8


def touched(index_list, positions):
    return jnp.any(index_list[:, :, :, None] == (positions // BLK)[None, None, None, :], axis=2)


def dense_device(separator, col_panels, row_panels, rows_list, cols_list, inverses):
    loc_rows = separator.shape[0]
    loc_cols = separator.shape[1]
    half = loc_cols // 2
    mine = lax.axis_index("leaf")
    row_ids = lax.axis_index("row") * loc_rows + jnp.arange(loc_rows, dtype=jnp.int32)
    subtrees = jnp.stack([mine])
    col_ids = lax.axis_index("col") * loc_cols + jnp.arange(loc_cols, dtype=jnp.int32)
    row_mask = touched(jnp.take(rows_list, subtrees, axis=0), row_ids)
    col_mask = touched(jnp.take(cols_list, subtrees, axis=0), col_ids)
    upper_all = lax.all_gather(row_panels, "row", axis=1, tiled=True)
    owner_all = jnp.arange(upper_all.shape[1], dtype=jnp.int32) // W
    keep_upper = jnp.take(col_mask, owner_all, axis=1)
    upper_all = jnp.where(keep_upper, upper_all, jnp.zeros_like(upper_all))
    piece = lax.all_gather(col_panels, "col", axis=2, tiled=True)
    owner = jnp.arange(piece.shape[2], dtype=jnp.int32) // W
    keep_lower = jnp.transpose(jnp.take(row_mask, owner, axis=1), (0, 2, 1))
    masked = jnp.where(keep_lower, piece, jnp.zeros_like(piece))
    update = jnp.einsum("srj,sjc->rc", masked, upper_all, preferred_element_type=jnp.float32)
    own_part = lax.dynamic_slice_in_dim(separator, mine * half, half, 1)
    both = lax.psum_scatter(update, "leaf", scatter_dimension=1, tiled=True)
    combined = own_part - both
    blocks = combined.reshape(loc_rows // W, W, half)
    factor = inverses.reshape(loc_rows // W, W, W)
    solved = jnp.einsum("bij,bjc->bic", factor, blocks, precision=lax.Precision.HIGHEST)
    return solved.reshape(loc_rows, half)


def mm(a, b):
    return jnp.dot(a.astype(jnp.bfloat16), b.astype(jnp.bfloat16), preferred_element_type=jnp.float32)


def grid_ids(shape):
    return lax.broadcasted_iota(jnp.int32, shape, 0), lax.broadcasted_iota(jnp.int32, shape, 1)


def ones_where(mask):
    return jnp.where(mask, jnp.float32(1), jnp.float32(0))


def list_mask(lists, held):
    leaves, kk, width = lists.shape
    lane = lax.broadcasted_iota(jnp.int32, (kk, BLK), 1)
    held[...] = jnp.zeros(held.shape, jnp.float32)
    for leaf in range(leaves):
        named = lists[leaf]
        hit = named[:, 0:1] == lane
        for s in range(1, width):
            hit = jnp.logical_or(hit, named[:, s:s + 1] == lane)
        held[leaf * LEAFROWS:leaf * LEAFROWS + kk, :] = ones_where(hit)
    return held[...]


def slice_counts(tr, sw, n_own):
    y, m = grid_ids((2 * LEAFROWS, 2 * LEAFROWS))
    same = jnp.logical_and(y // LEAFROWS == m // LEAFROWS, y % LEAFROWS < n_own)
    total = jnp.zeros(y.shape, jnp.float32)
    for t in range(tr):
        s = (y % LEAFROWS) * tr + t
        first = (m % LEAFROWS) * sw
        total = total + ones_where(same & (s >= first) & (s < first + sw))
    return total


def core_tails(counts, base):
    y, m = grid_ids((2 * LEAFROWS, 2 * LEAFROWS))
    past = jnp.maximum(counts - base, 0.0)
    chip = mm(ones_where(y % LEAFROWS == m % LEAFROWS), past)
    core = lax.broadcasted_iota(jnp.int32, past.shape, 0) // LEAFROWS
    carried = jnp.floor((chip + 1.0 - core.astype(jnp.float32)) * 0.5)
    return past, carried


def pack_kernel(n_row, n_col, tr, tc, hb, nb, kk, kinds, cols_s, rows_s, cols_v, rows_v, upper, lower,
                pu, pc, meta, flag_u, flag_l, held, pu_v, pc_v, sem_in, sem_out):
    r, c, mine = lax.axis_index("row"), lax.axis_index("col"), lax.axis_index("leaf")
    sw = W // BLK
    wb = 2 * hb
    n_ku, n_kl = -(-tr // sw) + 1, -(-tc // sw) + 1
    width_u, width_l = cols_v.shape[2], rows_v.shape[2]
    first_u, first_l = r * tr // sw, c * tc // sw

    @pl.loop(0, n_ku * (wb + 1))
    def _(i):
        flag_u[i] = jnp.int32(0)

    @pl.loop(0, n_kl * (nb + 1))
    def _(i):
        flag_l[i] = jnp.int32(0)

    for q in range(n_ku):
        at = (mine * kk + jnp.minimum(first_u + q, kk - 1)) * width_u
        for e in range(width_u):
            v = cols_s[at + e] - c * wb
            flag_u[q * (wb + 1) + jnp.where((v >= 0) & (v < wb), v, wb)] = jnp.int32(1)
    for q in range(n_kl):
        at = (mine * kk + jnp.minimum(first_l + q, kk - 1)) * width_l
        for e in range(width_l):
            v = rows_s[at + e] - r * nb
            flag_l[q * (nb + 1) + jnp.where((v >= 0) & (v < nb), v, nb)] = jnp.int32(1)

    def take_upper(i, n):
        t, j = i // wb, i % wb
        hit = flag_u[((r * tr + t) // sw - first_u) * (wb + 1) + j]

        @pl.when(hit > 0)
        def _():
            src = upper.at[0, pl.ds(pl.multiple_of(t * BLK, BLK), BLK), pl.ds(pl.multiple_of(j * BLK, BLK), BLK)]
            pltpu.make_async_copy(src, pu_v.at[n], sem_in).start()
        return n + hit

    def take_lower(i, n):
        t, j = i // nb, i % nb
        hit = flag_l[((c * tc + t) // sw - first_l) * (nb + 1) + j]

        @pl.when(hit > 0)
        def _():
            src = lower.at[0, pl.ds(pl.multiple_of(j * BLK, BLK), BLK), pl.ds(pl.multiple_of(t * BLK, BLK), BLK)]
            pltpu.make_async_copy(src, pc_v.at[n], sem_in).start()
        return n + hit

    n_u = lax.fori_loop(0, tr * wb, take_upper, jnp.int32(0))
    n_l = lax.fori_loop(0, tc * nb, take_lower, jnp.int32(0))

    row, lane = grid_ids((2 * LEAFROWS, BLK))
    J, x = grid_ids((BLK, BLK))
    cnt = mm(list_mask(cols_v, held), ones_where((J >= x * wb) & (J < (x + 1) * wb)))
    counts = mm(slice_counts(tr, sw, n_row), cnt)
    cnt_l = mm(list_mask(rows_v, held), ones_where((J >= x * nb) & (J < (x + 1) * nb)))
    counts_l = mm(slice_counts(tc, sw, n_col), cnt_l)
    base = kinds[0][0]
    past, carried = core_tails(counts, base)
    y, m = grid_ids((2 * LEAFROWS, 2 * LEAFROWS))
    same = y // LEAFROWS == m // LEAFROWS
    hop, src = y % LEAFROWS, m % LEAFROWS
    live = same & (hop <= n_row - 2) & (src < n_row)
    most = jnp.maximum(mm(ones_where(live & (src <= hop)), carried),
                       mm(ones_where(live & (src >= n_row - 1 - hop)), carried))
    hops = [jnp.max(jnp.where(row % LEAFROWS == h, most, 0.0)).astype(jnp.int32) for h in range(n_row - 1)]
    most_past = jnp.max(past).astype(jnp.int32)
    most_u = jnp.max(counts).astype(jnp.int32)
    most_l = jnp.max(counts_l).astype(jnp.int32)
    level = jnp.int32(0)
    for cap, over, carry, cap_l in kinds[:-1]:
        bad = most_l > cap_l
        if over:
            bad = jnp.logical_or(bad, most_past > over)
            for h in range(n_row - 1):
                bad = jnp.logical_or(bad, hops[h] > carry[h])
        else:
            bad = jnp.logical_or(bad, most_u > cap)
        level = level + bad.astype(jnp.int32)
    meta[0] = level
    for leaf in range(2):
        meta[1 + leaf] = jnp.sum(jnp.where((row == leaf * LEAFROWS + r) & (lane == c), past, 0.0)).astype(jnp.int32)

    @pl.loop(0, n_u + n_l)
    def _(i):
        pltpu.make_async_copy(pu.at[0], pu_v.at[0], sem_in).wait()

    step = 8

    def put(i, full, src, dst):
        at = pl.ds(jnp.minimum(i * step, full - step), step)
        return pltpu.make_async_copy(src.at[at], dst.at[at], sem_out)

    @pl.loop(0, (n_u + step - 1) // step)
    def _(i):
        put(i, pu.shape[0], pu_v, pu).start()

    @pl.loop(0, (n_l + step - 1) // step)
    def _(i):
        put(i, pc.shape[0], pc_v, pc).start()

    @pl.loop(0, (n_u + step - 1) // step + (n_l + step - 1) // step)
    def _(i):
        put(0, pu.shape[0], pu_v, pu).wait()


def gather_tables(n_row, n_col, tr, tc, hb, nb, base, full_u, full_l, carry_max, cols_v, rows_v, held, tab):
    r, c, mine = lax.axis_index("row"), lax.axis_index("col"), lax.axis_index("leaf")
    sw, wb = W // BLK, 2 * hb
    rows = 2 * LEAFROWS
    row, lane = grid_ids((rows, BLK))
    J, x = grid_ids((BLK, BLK))
    y, m = grid_ids((rows, rows))
    leaf, k = row // LEAFROWS, row % LEAFROWS
    before = ones_where(J < x)
    every = jnp.ones((BLK, BLK), jnp.float32)

    def pick(start, count):
        return ones_where((J == start + x) & (x < count))

    def slices(q, per, n_own):
        s = k * sw + q
        owner = jnp.zeros(s.shape, jnp.int32)
        for o in range(1, n_own):
            owner = owner + (s >= o * per).astype(jnp.int32)
        s_y = (y % LEAFROWS) * sw + q
        own_y = jnp.zeros(y.shape, jnp.int32)
        for o in range(1, n_own):
            own_y = own_y + (s_y >= o * per).astype(jnp.int32)
        weight = jnp.zeros(y.shape, jnp.float32)
        for other in range(sw):
            s_m = (m % LEAFROWS) * sw + other
            weight = weight + ones_where((y // LEAFROWS == m // LEAFROWS) & (s_m >= own_y * per) & (s_m < s_y))
        return owner, own_y, weight

    def store(mask, locs, n, at):
        rank = mm(mask, before)
        count = mm(mask, every)
        outs = [jnp.full(mask.shape, float(n), jnp.float32)] + [jnp.zeros(mask.shape, jnp.float32) for _ in locs]
        for i in range(n):
            sel = (mask > 0) & (rank == float(i))
            vals = [lane.astype(jnp.float32)] + locs
            for o in range(len(outs)):
                got = jnp.sum(jnp.where(sel, vals[o], 0.0), axis=1, keepdims=True)
                outs[o] = jnp.where((lane == i) & (count > float(i)), got, outs[o])
        outs[0] = jnp.where(lane == BLK // 2, count, outs[0])
        for o, v in enumerate(outs):
            tab[(at + o) * rows:(at + o + 1) * rows, :] = v.astype(jnp.int32)

    mask = list_mask(cols_v, held)
    chip = mm(mask, pick(c * wb, wb))
    cnt = mm(chip, every)
    rank = mm(chip, before)
    past, carried = core_tails(mm(slice_counts(tr, sw, n_row), cnt), base)
    half = pick(mine * hb, hb)
    mask_h, rank_h = mm(chip, half), mm(rank, half)
    locs = []
    for q in range(sw):
        owner, own_y, weight = slices(q, tr, n_row)
        p = mm(weight, cnt) + rank_h
        mine_y = m % LEAFROWS
        added = mm(ones_where((y // LEAFROWS == 1) & (m // LEAFROWS == 0) & (mine_y == own_y)), past)
        inner = ((own_y < mine_y) & (mine_y < r)) | ((r < mine_y) & (mine_y < own_y))
        passed = [mm(ones_where((m // LEAFROWS == a) & inner & (mine_y < n_row)), carried) for a in range(2)]
        e = p - base + added
        e_half = jnp.floor(e * 0.5)
        odd = e - 2.0 * e_half > 0.5
        plain = (owner * 2 + leaf).astype(jnp.float32) * full_u + p
        region = jnp.where(owner < r, n_row * 2 * full_u, n_row * 2 * full_u + 2 * carry_max).astype(jnp.float32)
        far = region + e_half + jnp.where(odd, passed[1] + carry_max, passed[0])
        locs.append(jnp.where((p < base) | (owner == r), plain, far))
    store(mask_h, locs, hb, 0)

    mask = list_mask(rows_v, held)
    mine_l = mm(mask, pick(r * nb, nb))
    cnt = mm(mine_l, every)
    rank = mm(mine_l, before)
    locs = []
    for q in range(sw):
        owner, _, weight = slices(q, tc, n_col)
        locs.append((leaf * n_col + owner).astype(jnp.float32) * full_l + mm(weight, cnt) + rank)
    store(mine_l, locs, nb, 1 + sw)


def comm_kernel(n_row, n_col, tr, tc, hb, nb, full_u, full_l, carry_max, kind,
                meta, cols_v, rows_v, pu, pc, g, gc, tab,
                held, tl, mv0, mv1, mo0, mo1, su, ru, sb, rb, sl, rl, sf, rf, sm, rm, sd, rd, so, st, rt, lo):
    base, over, carry, cap_l = kind
    mv, mo = (mv0, mv1), (mo0, mo1)
    r, c, mine = lax.axis_index("row"), lax.axis_index("col"), lax.axis_index("leaf")
    nl = pl.ds(0, cap_l)
    barrier = pltpu.get_barrier_semaphore()
    for d in (1, n_row - 1):
        pl.semaphore_signal(barrier, inc=1, device_id={"row": lax.rem(r + d, n_row)}, device_id_type=MESH)
    for d in range(1, n_col):
        pl.semaphore_signal(barrier, inc=1, device_id={"col": lax.rem(c + d, n_col)}, device_id_type=MESH)
    pl.semaphore_signal(barrier, inc=1, device_id={"leaf": 1 - mine}, device_id_type=MESH)
    pl.semaphore_wait(barrier, n_col + 2)

    cuts = [base * x // PARTS for x in range(PARTS + 1)]
    own_at = (r * 2 + mine) * full_u
    pair_id = {"leaf": 1 - mine}

    def blocks(shard, part, leaf):
        return g.at[pl.ds((shard * 2 + leaf) * full_u + cuts[part], cuts[part + 1] - cuts[part])]

    def line(way, step, part, shard, target):
        src = pu.at[pl.ds(cuts[part], cuts[part + 1] - cuts[part])] if step == 0 else blocks(shard, part, mine)
        return pltpu.make_async_remote_copy(
            src_ref=src, dst_ref=blocks(shard, part, mine), send_sem=su.at[way, step, part],
            recv_sem=ru.at[way, step, part], device_id={"row": target}, device_id_type=MESH)

    def line_send(way, step, part, act):
        goes = jnp.logical_and(r >= 1, r + step <= n_row - 1) if way == 0 else jnp.logical_and(r <= n_row - 2, r >= step)

        @pl.when(goes)
        def _():
            act(line(way, step, part, r + step if way == 0 else r - step, r - 1 if way == 0 else r + 1))

    def came(way, step):
        return r + 1 + step <= n_row - 1 if way == 0 else r >= 1 + step

    def shard_of(way, step):
        return r + 1 + step if way == 0 else r - 1 - step

    def line_wait(way, step, part):
        @pl.when(came(way, step))
        def _():
            line(way, step, part, shard_of(way, step), r + 1 if way == 0 else r - 1).wait_recv()

    def hand(way, step, part, leaf):
        at = blocks(shard_of(way, step), part, leaf)
        return pltpu.make_async_remote_copy(
            src_ref=at, dst_ref=at, send_sem=sb.at[way, step, part], recv_sem=rb.at[way, step, part],
            device_id=pair_id, device_id_type=MESH)

    def hand_if(way, step, part, leaf, act):
        @pl.when(came(way, step))
        def _():
            act(hand(way, step, part, leaf))

    def hand_own(leaf):
        at = g.at[pl.ds((r * 2 + leaf) * full_u, base + over)]
        return pltpu.make_async_remote_copy(
            src_ref=pu.at[pl.ds(0, base + over)] if leaf is mine else at, dst_ref=at, send_sem=so.at[0],
            recv_sem=so.at[1], device_id=pair_id, device_id_type=MESH)

    def across(d, slot):
        return pltpu.make_async_remote_copy(
            src_ref=pc.at[nl], dst_ref=gc.at[slot, nl], send_sem=sl.at[d], recv_sem=rl.at[d],
            device_id={"col": lax.rem(c + d, n_col)}, device_id_type=MESH)

    def from_slot(d, leaf):
        return leaf * n_col + lax.rem(c + n_col - d, n_col)

    def pair(d, leaf):
        slot = from_slot(d, leaf)
        return pltpu.make_async_remote_copy(
            src_ref=pc.at[nl] if d == 0 else gc.at[slot, nl], dst_ref=gc.at[slot, nl],
            send_sem=sf.at[d], recv_sem=rf.at[d], device_id=pair_id, device_id_type=MESH)

    def tail(leaf):
        return pltpu.make_async_remote_copy(
            src_ref=pu.at[pl.ds(base, over)], dst_ref=tl.at[pl.ds(leaf * over, over)], send_sem=st.at[0],
            recv_sem=st.at[1], device_id=pair_id, device_id_type=MESH)

    tail_here = pltpu.make_async_copy(pu.at[pl.ds(base, over)], tl.at[pl.ds(mine * over, over)], lo.at[2]) if over else None
    own_here = pltpu.make_async_copy(pu.at[pl.ds(0, base + over)], g.at[pl.ds(own_at, base + over)], lo.at[0])
    low_here = pltpu.make_async_copy(pc.at[nl], gc.at[mine * n_col + c, nl], lo.at[1])

    def carry_copy(way, h, target):
        n = pl.ds(0, carry[h])
        return pltpu.make_async_remote_copy(
            src_ref=mo[way].at[n], dst_ref=mv[way].at[n], send_sem=sm.at[way], recv_sem=rm.at[way],
            device_id={"row": target}, device_id_type=MESH)

    def carry_at(way, h, leaf):
        start = n_row * 2 * full_u + (2 * carry_max if way == 0 else 0) + leaf * carry_max
        return g.at[pl.ds(start, carry[h])]

    def carry_hand(way, h, leaf):
        at = carry_at(way, h, leaf)
        return pltpu.make_async_remote_copy(
            src_ref=mv[way].at[pl.ds(0, carry[h])] if leaf is mine else at, dst_ref=at, send_sem=sd.at[way],
            recv_sem=rd.at[way], device_id=pair_id, device_id_type=MESH)

    def carry_here(way, h):
        return pltpu.make_async_copy(mv[way].at[pl.ds(0, carry[h])], carry_at(way, h, mine), lo.at[3 + way])

    def next_row(way):
        return r - 1 if way == 0 else r + 1

    def merge(way, h):
        t0, t1 = meta[1], meta[2]
        n_here = (t0 + t1 + 1 - mine) // 2

        @pl.loop(0, carry[h])
        def _(i):
            e = 2 * i + mine
            own = tl[jnp.clip(jnp.where(e < t0, e, over + e - t0), 0, 2 * over - 1)]
            if h > 0:
                prev = mv[way][jnp.clip(i - n_here, 0, carry[h - 1] - 1)]
                own = jnp.where(i < n_here, own, prev)
            mo[way][i] = own

    def at_hop(way, h):
        return n_row - 1 - h if way == 0 else h

    if over:
        tail(mine).start()
        tail_here.start()
    for part in range(PARTS):
        for way in range(2):
            line_send(way, 0, part, lambda copy: copy.start())
    for d in range(1, n_col):
        across(d, mine * n_col + c).start()
    pair(0, mine).start()
    hand_own(mine).start()
    own_here.start()
    low_here.start()
    if over:
        tail(1 - mine).wait_recv()
        tail_here.wait()
        for way in range(2):
            @pl.when(r == at_hop(way, 0))
            def _(way=way):
                merge(way, 0)
                carry_copy(way, 0, next_row(way)).start()
    gather_tables(n_row, n_col, tr, tc, hb, nb, base, full_u, full_l, carry_max, cols_v, rows_v, held, tab)
    for step in range(n_row - 1):
        for part in range(PARTS):
            for way in range(2):
                line_wait(way, step, part)
                if step < n_row - 2:
                    line_send(way, step + 1, part, lambda copy: copy.start())
                hand_if(way, step, part, mine, lambda copy: copy.start())
        if over:
            for way in range(2):
                @pl.when(r == at_hop(way, step + 1))
                def _(way=way):
                    carry_copy(way, step, next_row(1 - way)).wait_recv()
                    if step < n_row - 2:
                        merge(way, step + 1)
                    carry_hand(way, step, mine).start()
                    carry_here(way, step).start()
                    if step < n_row - 2:
                        carry_copy(way, step + 1, next_row(way)).start()
        if step == 0:
            for d in range(1, n_col):
                across(d, from_slot(d, mine)).wait_recv()
                pair(d, mine).start()
    for d in range(n_col):
        pair(d, 1 - mine).wait_recv()
    hand_own(1 - mine).wait_recv()
    for step in range(n_row - 1):
        for part in range(PARTS):
            for way in range(2):
                hand_if(way, step, part, 1 - mine, lambda copy: copy.wait_recv())
    if over:
        for step in range(n_row - 1):
            for way in range(2):
                @pl.when(r == at_hop(way, step + 1))
                def _(way=way):
                    carry_hand(way, step, 1 - mine).wait_recv()
                    carry_hand(way, step, mine).wait_send()
                    carry_here(way, step).wait()

                @pl.when(r == at_hop(way, step))
                def _(way=way):
                    carry_copy(way, step, next_row(way)).wait_send()
        tail(mine).wait_send()
    own_here.wait()
    low_here.wait()
    hand_own(mine).wait_send()
    for d in range(n_col):
        pair(d, mine).wait_send()
    for d in range(1, n_col):
        across(d, mine * n_col + c).wait_send()
    for step in range(n_row - 1):
        for part in range(PARTS):
            for way in range(2):
                line_send(way, step, part, lambda copy: copy.wait_send())
                hand_if(way, step, part, mine, lambda copy: copy.wait_send())


def split(x):
    hi = x.astype(jnp.bfloat16)
    return hi, (x - hi.astype(jnp.float32)).astype(jnp.bfloat16)


GROUP = 4


def solve_kernel(n_row, n_col, hb, nb, kk, full_l, tab, sep, inv, g, gc, out, low, up, acc, prod, sem, sep_sem):
    sw = W // BLK
    half, loc_rows = hb * BLK, nb * BLK
    rows_of = 2 * LEAFROWS
    b = pl.program_id(0)

    @pl.when(b == 0)
    def _():
        mine = lax.axis_index("leaf")
        load = pltpu.make_async_copy(
            sep.at[:, pl.ds(pl.multiple_of(mine * half, half), half)],
            acc.at[pl.ds(0, loc_rows), pl.ds(0, half)], sep_sem)
        counts = []
        total = jnp.int32(0)
        for leaf in range(2):
            for k in range(kk):
                m, at_m = leaf * kk + k, leaf * LEAFROWS + k
                n_u, n_l = tab[at_m, BLK // 2], tab[(1 + sw) * rows_of + at_m, BLK // 2]

                @pl.loop(0, n_u)
                def _(n, m=m, at_m=at_m):
                    at = pl.ds(pl.multiple_of(n * BLK, BLK), BLK)
                    for q in range(sw):
                        src = g.at[tab[(1 + q) * rows_of + at_m, n]]
                        pltpu.make_async_copy(src, up.at[m, pl.ds(q * BLK, BLK), at], sem).start()

                @pl.loop(0, n_l)
                def _(n, m=m, at_m=at_m):
                    at = pl.ds(pl.multiple_of(n * BLK, BLK), BLK)
                    for q in range(sw):
                        p = tab[(2 + sw + q) * rows_of + at_m, n]
                        src = gc.at[p // full_l, p % full_l]
                        pltpu.make_async_copy(src, low.at[m, at, pl.ds(q * BLK, BLK)], sem).start()

                counts.append((n_u, n_l))
                total = total + (n_u + n_l) * sw

        load.start()

        @pl.loop(0, total)
        def _(n):
            pltpu.make_async_copy(g.at[0], low.at[0, pl.ds(0, BLK), pl.ds(0, BLK)], sem).wait()

        load.wait()
        wide = GROUP * BLK
        for m, (n_u, n_l) in enumerate(counts):
            at_m = m // kk * LEAFROWS + m % kk

            @pl.loop(0, (n_l + GROUP - 1) // GROUP)
            def _(x, m=m, at_m=at_m, n_u=n_u, n_l=n_l):
                rows = pl.ds(pl.multiple_of(x * wide, wide), wide)

                @pl.loop(0, (n_u + GROUP - 1) // GROUP)
                def _(y):
                    cols = pl.ds(pl.multiple_of(y * wide, wide), wide)
                    prod[...] = jnp.dot(low[m, rows, :], up[m, :, cols], preferred_element_type=jnp.float32)
                    for i in range(GROUP):
                        row = tab[(1 + sw) * rows_of + at_m, x * GROUP + i]

                        @pl.when(row < nb)
                        def _(i=i, row=row):
                            to = pl.ds(pl.multiple_of(row * BLK, BLK), BLK)
                            for j in range(GROUP):
                                col = tab[at_m, y * GROUP + j]
                                at = pl.ds(pl.multiple_of(col * BLK, BLK), BLK)
                                acc[to, at] -= prod[i * BLK:(i + 1) * BLK, j * BLK:(j + 1) * BLK]

    tile = min(512, half)
    rows = pl.ds(pl.multiple_of(b * W, W), W)
    f_hi, f_lo = split(inv[...])
    for n in range(half // tile):
        at = pl.ds(n * tile, tile)
        hi, lo = split(acc[rows, at])
        out[:, at] = (jnp.dot(f_hi, hi, preferred_element_type=jnp.float32)
                      + (jnp.dot(f_hi, lo, preferred_element_type=jnp.float32)
                         + jnp.dot(f_lo, hi, preferred_element_type=jnp.float32)))


def solve_call(n_row, n_col, hb, nb, kk, full_l):
    hbm = pl.BlockSpec(memory_space=pl.ANY)
    half, loc_rows = hb * BLK, nb * BLK
    hg, ng = -(-hb // GROUP) * GROUP, -(-nb // GROUP) * GROUP
    return pl.pallas_call(
        functools.partial(solve_kernel, n_row, n_col, hb, nb, kk, full_l),
        out_shape=jax.ShapeDtypeStruct((loc_rows, half), jnp.float32),
        grid_spec=pltpu.PrefetchScalarGridSpec(
            num_scalar_prefetch=1, grid=(loc_rows // W,),
            in_specs=[hbm, pl.BlockSpec((W, W), lambda i, t: (i, 0)), hbm, hbm],
            out_specs=pl.BlockSpec((W, half), lambda i, t: (i, 0)),
            scratch_shapes=[pltpu.VMEM((2 * kk, ng * BLK, W), jnp.bfloat16),
                            pltpu.VMEM((2 * kk, W, hg * BLK), jnp.bfloat16),
                            pltpu.VMEM((loc_rows, half + BLK), jnp.float32),
                            pltpu.VMEM((GROUP * BLK, GROUP * BLK), jnp.float32),
                            pltpu.SemaphoreType.DMA, pltpu.SemaphoreType.DMA]),
        compiler_params=pltpu.CompilerParams(vmem_limit_bytes=58 * 2**20),
    )


def kinds_of(full_u, full_l, n_row):
    base, over = -(-full_u * 20 // 96), -(-full_u * 24 // 96)
    found = []
    for last, inner, first, low in ((12, 12, 12, 22), (14, 14, 14, 24), (15, 15, 14, 24), (16, 16, 14, 24), (17, 16, 14, 24),
                                    (18, 17, 14, 24), (20, 18, 16, 26), (22, 19, 16, 26), (26, 22, 18, 28), (34, 28, 20, 28)):
        sizes = [first] + [inner] * (n_row - 3) + [last]
        found.append((base, over, tuple(-(-full_u * v // 96) for v in sizes[:n_row - 1]), -(-full_l * low // 48)))
    found.append((-(-full_u * 48 // 96), 0, None, -(-full_l * 40 // 48)))
    found.append((full_u, 0, None, full_l))
    return found


def sparse_device(n_row, n_col, separator, col_panels, row_panels, rows_list, cols_list, inverses):
    loc_rows, loc_cols = separator.shape
    half = loc_cols // 2
    tr, tc = row_panels.shape[1] // BLK, col_panels.shape[2] // BLK
    hb, nb = half // BLK, loc_rows // BLK
    kk = rows_list.shape[1]
    sw = W // BLK
    full_u, full_l = 2 * tr * hb, tc * nb
    kinds = kinds_of(full_u, full_l, n_row)
    carry_max = max(max(kind[2]) for kind in kinds if kind[2])
    over = kinds[0][1]

    block = (BLK, BLK)
    bf16 = jnp.bfloat16
    hbm = pl.BlockSpec(memory_space=pl.ANY)
    vmem = pl.BlockSpec(memory_space=pltpu.VMEM)
    smem = pl.BlockSpec(memory_space=pltpu.SMEM)
    dma = pltpu.SemaphoreType.DMA
    n_ku, n_kl = -(-tr // sw) + 1, -(-tc // sw) + 1
    pu, pc, meta = pl.pallas_call(
        functools.partial(pack_kernel, n_row, n_col, tr, tc, hb, nb, kk, kinds),
        out_shape=(jax.ShapeDtypeStruct((full_u,) + block, bf16), jax.ShapeDtypeStruct((full_l,) + block, bf16),
                   jax.ShapeDtypeStruct((3,), jnp.int32)),
        in_specs=[smem, smem, vmem, vmem, hbm, hbm], out_specs=(hbm, hbm, smem),
        scratch_shapes=[pltpu.SMEM((n_ku * (2 * hb + 1),), jnp.int32), pltpu.SMEM((n_kl * (nb + 1),), jnp.int32),
                        pltpu.VMEM((2 * LEAFROWS, BLK), jnp.float32),
                        pltpu.VMEM((full_u,) + block, bf16), pltpu.VMEM((full_l,) + block, bf16), dma, dma],
        compiler_params=pltpu.CompilerParams(vmem_limit_bytes=16 * 2**20),
        name="pack",
    )(cols_list.reshape(-1), rows_list.reshape(-1), cols_list, rows_list, row_panels, col_panels)

    n_all = n_row * 2 * full_u + 4 * carry_max
    tab_rows = 2 * (1 + sw) * 2 * LEAFROWS

    def exchange(which):
        def run(*args):
            return pl.pallas_call(
                functools.partial(comm_kernel, n_row, n_col, tr, tc, hb, nb, full_u, full_l, carry_max, kinds[which]),
                out_shape=(jax.ShapeDtypeStruct((n_all,) + block, bf16),
                           jax.ShapeDtypeStruct((2 * n_col, full_l) + block, bf16),
                           jax.ShapeDtypeStruct((tab_rows, BLK), jnp.int32)),
                in_specs=[smem, vmem, vmem, hbm, hbm], out_specs=(hbm, hbm, vmem),
                scratch_shapes=[pltpu.VMEM((2 * LEAFROWS, BLK), jnp.float32), pltpu.VMEM((2 * over,) + block, bf16),
                                *[pltpu.VMEM((carry_max,) + block, bf16)] * 4]
                + [dma((2, n_row, PARTS))] * 4 + [dma((n_col,))] * 4 + [dma((2,))] * 7 + [dma((5,))],
                compiler_params=pltpu.CompilerParams(collective_id=which, has_side_effects=True,
                                                     vmem_limit_bytes=16 * 2**20),
                name="exchange%d" % which,
            )(*args)
        return run

    g, gc, tab = lax.switch(meta[0], [exchange(i) for i in range(len(kinds))], meta, cols_list, rows_list, pu, pc)
    return solve_call(n_row, n_col, hb, nb, kk, full_l)(tab, separator, inverses, g, gc)


def solution(mesh):
    placed = (
        P("row", "col"),
        P("leaf", "row", "col"),
        P("leaf", "row", "col"),
        P(),
        P(),
        P("row", None),
    )
    n_row, n_col = mesh.shape["row"], mesh.shape["col"]

    def per_device(separator, col_panels, row_panels, *rest):
        whole = separator.shape[1] % (2 * W) == 0 and separator.shape[0] % W == 0
        fits = (rest[0].shape[1] <= LEAFROWS and 3 <= n_row <= LEAFROWS and n_col <= LEAFROWS
                and n_row * separator.shape[0] <= BLK * BLK and n_col * separator.shape[1] <= BLK * BLK)
        if whole and row_panels.shape[1] % BLK == 0 and col_panels.shape[2] % BLK == 0 and mesh.shape["leaf"] == 2 and fits:
            return sparse_device(n_row, n_col, separator, col_panels, row_panels, *rest)
        return dense_device(separator, col_panels, row_panels, *rest)

    return jax.shard_map(
        per_device, mesh=mesh, in_specs=placed, out_specs=P("row", ("col", "leaf")), check_vma=False
    )
```

```python
import functools

import jax
import jax.numpy as jnp
from jax import lax
from jax.experimental import pallas as pl
from jax.experimental.pallas import tpu as pltpu
from jax.sharding import PartitionSpec as P

W = 256
BLK = 128
MESH = pl.DeviceIdType.MESH
PARTS = 2
LEAFROWS = 8


def touched(index_list, positions):
    return jnp.any(index_list[:, :, :, None] == (positions // BLK)[None, None, None, :], axis=2)


def dense_device(separator, col_panels, row_panels, rows_list, cols_list, inverses):
    loc_rows = separator.shape[0]
    loc_cols = separator.shape[1]
    half = loc_cols // 2
    mine = lax.axis_index("leaf")
    row_ids = lax.axis_index("row") * loc_rows + jnp.arange(loc_rows, dtype=jnp.int32)
    subtrees = jnp.stack([mine])
    col_ids = lax.axis_index("col") * loc_cols + jnp.arange(loc_cols, dtype=jnp.int32)
    row_mask = touched(jnp.take(rows_list, subtrees, axis=0), row_ids)
    col_mask = touched(jnp.take(cols_list, subtrees, axis=0), col_ids)
    upper_all = lax.all_gather(row_panels, "row", axis=1, tiled=True)
    owner_all = jnp.arange(upper_all.shape[1], dtype=jnp.int32) // W
    keep_upper = jnp.take(col_mask, owner_all, axis=1)
    upper_all = jnp.where(keep_upper, upper_all, jnp.zeros_like(upper_all))
    piece = lax.all_gather(col_panels, "col", axis=2, tiled=True)
    owner = jnp.arange(piece.shape[2], dtype=jnp.int32) // W
    keep_lower = jnp.transpose(jnp.take(row_mask, owner, axis=1), (0, 2, 1))
    masked = jnp.where(keep_lower, piece, jnp.zeros_like(piece))
    update = jnp.einsum("srj,sjc->rc", masked, upper_all, preferred_element_type=jnp.float32)
    own_part = lax.dynamic_slice_in_dim(separator, mine * half, half, 1)
    both = lax.psum_scatter(update, "leaf", scatter_dimension=1, tiled=True)
    combined = own_part - both
    blocks = combined.reshape(loc_rows // W, W, half)
    factor = inverses.reshape(loc_rows // W, W, W)
    solved = jnp.einsum("bij,bjc->bic", factor, blocks, precision=lax.Precision.HIGHEST)
    return solved.reshape(loc_rows, half)


def mm(a, b):
    return jnp.dot(a.astype(jnp.bfloat16), b.astype(jnp.bfloat16), preferred_element_type=jnp.float32)


def grid_ids(shape):
    return lax.broadcasted_iota(jnp.int32, shape, 0), lax.broadcasted_iota(jnp.int32, shape, 1)


def ones_where(mask):
    return jnp.where(mask, jnp.float32(1), jnp.float32(0))


def list_mask(lists, held):
    leaves, kk, width = lists.shape
    lane = lax.broadcasted_iota(jnp.int32, (1, BLK), 1)
    held[...] = jnp.zeros(held.shape, jnp.float32)
    for leaf in range(leaves):
        for k in range(kk):
            hit = lane == lists[leaf, k, 0]
            for e in range(1, width):
                hit = jnp.logical_or(hit, lane == lists[leaf, k, e])
            held[leaf * LEAFROWS + k:leaf * LEAFROWS + k + 1, :] = ones_where(hit)
    return held[...]


def slice_counts(tr, sw, n_own):
    y, m = grid_ids((2 * LEAFROWS, 2 * LEAFROWS))
    same = jnp.logical_and(y // LEAFROWS == m // LEAFROWS, y % LEAFROWS < n_own)
    total = jnp.zeros(y.shape, jnp.float32)
    for t in range(tr):
        s = (y % LEAFROWS) * tr + t
        first = (m % LEAFROWS) * sw
        total = total + ones_where(same & (s >= first) & (s < first + sw))
    return total


def core_tails(counts, base):
    y, m = grid_ids((2 * LEAFROWS, 2 * LEAFROWS))
    past = jnp.maximum(counts - base, 0.0)
    chip = mm(ones_where(y % LEAFROWS == m % LEAFROWS), past)
    core = lax.broadcasted_iota(jnp.int32, past.shape, 0) // LEAFROWS
    carried = jnp.floor((chip + 1.0 - core.astype(jnp.float32)) * 0.5)
    return past, carried


def pack_kernel(n_row, n_col, tr, tc, hb, nb, kk, kinds, cols_s, rows_s, upper, lower,
                pu, pc, meta, named_u, named_l, flag_u, flag_l, pu_v, pc_v, sem_in, sem_out):
    r, c, mine = lax.axis_index("row"), lax.axis_index("col"), lax.axis_index("leaf")
    sw = W // BLK
    wb = 2 * hb
    n_ku, n_kl = -(-tr // sw) + 1, -(-tc // sw) + 1
    width_u, width_l = cols_s.shape[2], rows_s.shape[2]
    first_u, first_l = r * tr // sw, c * tc // sw

    @pl.loop(0, n_ku * (wb + 1))
    def _(i):
        flag_u[i] = jnp.int32(0)

    @pl.loop(0, n_kl * (nb + 1))
    def _(i):
        flag_l[i] = jnp.int32(0)

    for q in range(n_ku):
        at = jnp.minimum(first_u + q, kk - 1)
        for e in range(width_u):
            v = cols_s[mine, at, e] - c * wb
            flag_u[q * (wb + 1) + jnp.where((v >= 0) & (v < wb), v, wb)] = jnp.int32(1)
    for q in range(n_kl):
        at = jnp.minimum(first_l + q, kk - 1)
        for e in range(width_l):
            v = rows_s[mine, at, e] - r * nb
            flag_l[q * (nb + 1) + jnp.where((v >= 0) & (v < nb), v, nb)] = jnp.int32(1)

    n_u = n_l = jnp.int32(0)
    for t in range(tr):
        flags = ((r * tr + t) // sw - first_u) * (wb + 1)

        def take_upper(j, n, t=t, flags=flags):
            hit = flag_u[flags + j]

            @pl.when(hit > 0)
            def _():
                src = upper.at[0, pl.ds(t * BLK, BLK), pl.ds(pl.multiple_of(j * BLK, BLK), BLK)]
                pltpu.make_async_copy(src, pu_v.at[n], sem_in).start()
            return n + hit

        n_u = lax.fori_loop(0, wb, take_upper, n_u)
    for t in range(tc):
        flags = ((c * tc + t) // sw - first_l) * (nb + 1)

        def take_lower(j, n, t=t, flags=flags):
            hit = flag_l[flags + j]

            @pl.when(hit > 0)
            def _():
                src = lower.at[0, pl.ds(pl.multiple_of(j * BLK, BLK), BLK), pl.ds(t * BLK, BLK)]
                pltpu.make_async_copy(src, pc_v.at[n], sem_in).start()
            return n + hit

        n_l = lax.fori_loop(0, nb, take_lower, n_l)

    row, lane = grid_ids((2 * LEAFROWS, BLK))
    J, x = grid_ids((BLK, BLK))
    cnt = mm(list_mask(cols_s, named_u), ones_where((J >= x * wb) & (J < (x + 1) * wb)))
    counts = mm(slice_counts(tr, sw, n_row), cnt)
    cnt_l = mm(list_mask(rows_s, named_l), ones_where((J >= x * nb) & (J < (x + 1) * nb)))
    counts_l = mm(slice_counts(tc, sw, n_col), cnt_l)
    base = kinds[0][0]
    past, carried = core_tails(counts, base)
    y, m = grid_ids((2 * LEAFROWS, 2 * LEAFROWS))
    same = y // LEAFROWS == m // LEAFROWS
    hop, src = y % LEAFROWS, m % LEAFROWS
    live = same & (hop <= n_row - 2) & (src < n_row)
    most = jnp.maximum(mm(ones_where(live & (src <= hop)), carried),
                       mm(ones_where(live & (src >= n_row - 1 - hop)), carried))
    hops = [jnp.max(jnp.where(row % LEAFROWS == h, most, 0.0)).astype(jnp.int32) for h in range(n_row - 1)]
    most_past = jnp.max(past).astype(jnp.int32)
    most_u = jnp.max(counts).astype(jnp.int32)
    most_l = jnp.max(counts_l).astype(jnp.int32)
    level = jnp.int32(0)
    for cap, over, carry, cap_l in kinds[:-1]:
        bad = most_l > cap_l
        if over:
            bad = jnp.logical_or(bad, most_past > over)
            for h in range(n_row - 1):
                bad = jnp.logical_or(bad, hops[h] > carry[h])
        else:
            bad = jnp.logical_or(bad, most_u > cap)
        level = level + bad.astype(jnp.int32)
    meta[0] = level
    for leaf in range(2):
        meta[1 + leaf] = jnp.sum(jnp.where((row == leaf * LEAFROWS + r) & (lane == c), past, 0.0)).astype(jnp.int32)

    @pl.loop(0, n_u + n_l)
    def _(i):
        pltpu.make_async_copy(pu.at[0], pu_v.at[0], sem_in).wait()

    step = 8

    def put(i, full, src, dst):
        at = pl.ds(jnp.minimum(i * step, full - step), step)
        return pltpu.make_async_copy(src.at[at], dst.at[at], sem_out)

    @pl.loop(0, (n_u + step - 1) // step)
    def _(i):
        put(i, pu.shape[0], pu_v, pu).start()

    @pl.loop(0, (n_l + step - 1) // step)
    def _(i):
        put(i, pc.shape[0], pc_v, pc).start()

    @pl.loop(0, (n_u + step - 1) // step + (n_l + step - 1) // step)
    def _(i):
        put(0, pu.shape[0], pu_v, pu).wait()


def gather_tables(n_row, n_col, tr, tc, hb, nb, base, full_u, full_l, carry_max, named_u, named_l, tab):
    r, c, mine = lax.axis_index("row"), lax.axis_index("col"), lax.axis_index("leaf")
    sw, wb = W // BLK, 2 * hb
    rows = 2 * LEAFROWS
    row, lane = grid_ids((rows, BLK))
    J, x = grid_ids((BLK, BLK))
    y, m = grid_ids((rows, rows))
    leaf, k = row // LEAFROWS, row % LEAFROWS
    before = ones_where(J < x)
    every = jnp.ones((BLK, BLK), jnp.float32)

    def pick(start, count):
        return ones_where((J == start + x) & (x < count))

    def slices(q, per, n_own):
        s = k * sw + q
        owner = jnp.zeros(s.shape, jnp.int32)
        for o in range(1, n_own):
            owner = owner + (s >= o * per).astype(jnp.int32)
        s_y = (y % LEAFROWS) * sw + q
        own_y = jnp.zeros(y.shape, jnp.int32)
        for o in range(1, n_own):
            own_y = own_y + (s_y >= o * per).astype(jnp.int32)
        weight = jnp.zeros(y.shape, jnp.float32)
        for other in range(sw):
            s_m = (m % LEAFROWS) * sw + other
            weight = weight + ones_where((y // LEAFROWS == m // LEAFROWS) & (s_m >= own_y * per) & (s_m < s_y))
        return owner, own_y, weight

    def store(mask, locs, n, at):
        rank = mm(mask, before)
        count = mm(mask, every)
        outs = [jnp.full(mask.shape, float(n), jnp.float32)] + [jnp.zeros(mask.shape, jnp.float32) for _ in locs]
        for i in range(n):
            sel = (mask > 0) & (rank == float(i))
            vals = [lane.astype(jnp.float32)] + locs
            for o in range(len(outs)):
                got = jnp.sum(jnp.where(sel, vals[o], 0.0), axis=1, keepdims=True)
                outs[o] = jnp.where((lane == i) & (count > float(i)), got, outs[o])
        outs[0] = jnp.where(lane == BLK // 2, count, outs[0])
        for o, v in enumerate(outs):
            tab[(at + o) * rows:(at + o + 1) * rows, :] = v.astype(jnp.int32)

    mask = named_u[...]
    chip = mm(mask, pick(c * wb, wb))
    cnt = mm(chip, every)
    rank = mm(chip, before)
    past, carried = core_tails(mm(slice_counts(tr, sw, n_row), cnt), base)
    half = pick(mine * hb, hb)
    mask_h, rank_h = mm(chip, half), mm(rank, half)
    locs = []
    for q in range(sw):
        owner, own_y, weight = slices(q, tr, n_row)
        p = mm(weight, cnt) + rank_h
        mine_y = m % LEAFROWS
        added = mm(ones_where((y // LEAFROWS == 1) & (m // LEAFROWS == 0) & (mine_y == own_y)), past)
        inner = ((own_y < mine_y) & (mine_y < r)) | ((r < mine_y) & (mine_y < own_y))
        passed = [mm(ones_where((m // LEAFROWS == a) & inner & (mine_y < n_row)), carried) for a in range(2)]
        e = p - base + added
        e_half = jnp.floor(e * 0.5)
        odd = e - 2.0 * e_half > 0.5
        plain = (owner * 2 + leaf).astype(jnp.float32) * full_u + p
        region = jnp.where(owner < r, n_row * 2 * full_u, n_row * 2 * full_u + 2 * carry_max).astype(jnp.float32)
        far = region + e_half + jnp.where(odd, passed[1] + carry_max, passed[0])
        locs.append(jnp.where((p < base) | (owner == r), plain, far))
    store(mask_h, locs, hb, 0)

    mask = named_l[...]
    mine_l = mm(mask, pick(r * nb, nb))
    cnt = mm(mine_l, every)
    rank = mm(mine_l, before)
    locs = []
    for q in range(sw):
        owner, _, weight = slices(q, tc, n_col)
        locs.append((leaf * n_col + owner).astype(jnp.float32) * full_l + mm(weight, cnt) + rank)
    store(mine_l, locs, nb, 1 + sw)


def comm_kernel(n_row, n_col, tr, tc, hb, nb, full_u, full_l, carry_max, kind,
                meta, named_u, named_l, pu, pc, sep, g, gc, tab, acc,
                tl, mv0, mv1, mo0, mo1, su, ru, sb, rb, sl, rl, sf, rf, sm, rm, sd, rd, so, st, rt, lo):
    base, over, carry, cap_l = kind
    mv, mo = (mv0, mv1), (mo0, mo1)
    r, c, mine = lax.axis_index("row"), lax.axis_index("col"), lax.axis_index("leaf")
    nl = pl.ds(0, cap_l)

    def low_slot(slot):
        return pl.ds(slot * full_l, cap_l)

    barrier = pltpu.get_barrier_semaphore()
    for d in (1, n_row - 1):
        pl.semaphore_signal(barrier, inc=1, device_id={"row": lax.rem(r + d, n_row)}, device_id_type=MESH)
    for d in range(1, n_col):
        pl.semaphore_signal(barrier, inc=1, device_id={"col": lax.rem(c + d, n_col)}, device_id_type=MESH)
    pl.semaphore_signal(barrier, inc=1, device_id={"leaf": 1 - mine}, device_id_type=MESH)
    pl.semaphore_wait(barrier, n_col + 2)

    cuts = [base * x // PARTS for x in range(PARTS + 1)]
    own_at = (r * 2 + mine) * full_u
    pair_id = {"leaf": 1 - mine}

    def blocks(shard, part, leaf):
        return g.at[pl.ds((shard * 2 + leaf) * full_u + cuts[part], cuts[part + 1] - cuts[part])]

    def line(way, step, part, shard, target):
        src = pu.at[pl.ds(cuts[part], cuts[part + 1] - cuts[part])] if step == 0 else blocks(shard, part, mine)
        return pltpu.make_async_remote_copy(
            src_ref=src, dst_ref=blocks(shard, part, mine), send_sem=su.at[way, step, part],
            recv_sem=ru.at[way, step, part], device_id={"row": target}, device_id_type=MESH)

    def line_send(way, step, part, act):
        goes = jnp.logical_and(r >= 1, r + step <= n_row - 1) if way == 0 else jnp.logical_and(r <= n_row - 2, r >= step)

        @pl.when(goes)
        def _():
            act(line(way, step, part, r + step if way == 0 else r - step, r - 1 if way == 0 else r + 1))

    def came(way, step):
        return r + 1 + step <= n_row - 1 if way == 0 else r >= 1 + step

    def shard_of(way, step):
        return r + 1 + step if way == 0 else r - 1 - step

    def line_wait(way, step, part):
        @pl.when(came(way, step))
        def _():
            line(way, step, part, shard_of(way, step), r + 1 if way == 0 else r - 1).wait_recv()

    def hand(way, step, part, leaf):
        at = blocks(shard_of(way, step), part, leaf)
        return pltpu.make_async_remote_copy(
            src_ref=at, dst_ref=at, send_sem=sb.at[way, step, part], recv_sem=rb.at[way, step, part],
            device_id=pair_id, device_id_type=MESH)

    def hand_if(way, step, part, leaf, act):
        @pl.when(came(way, step))
        def _():
            act(hand(way, step, part, leaf))

    def hand_own(leaf):
        at = g.at[pl.ds((r * 2 + leaf) * full_u, base + over)]
        return pltpu.make_async_remote_copy(
            src_ref=pu.at[pl.ds(0, base + over)] if leaf is mine else at, dst_ref=at, send_sem=so.at[0],
            recv_sem=so.at[1], device_id=pair_id, device_id_type=MESH)

    def across(d, slot):
        return pltpu.make_async_remote_copy(
            src_ref=pc.at[nl], dst_ref=gc.at[low_slot(slot)], send_sem=sl.at[d], recv_sem=rl.at[d],
            device_id={"col": lax.rem(c + d, n_col)}, device_id_type=MESH)

    def from_slot(d, leaf):
        return leaf * n_col + lax.rem(c + n_col - d, n_col)

    def pair(d, leaf):
        slot = from_slot(d, leaf)
        return pltpu.make_async_remote_copy(
            src_ref=pc.at[nl] if d == 0 else gc.at[low_slot(slot)], dst_ref=gc.at[low_slot(slot)],
            send_sem=sf.at[d], recv_sem=rf.at[d], device_id=pair_id, device_id_type=MESH)

    def tail(leaf):
        return pltpu.make_async_remote_copy(
            src_ref=pu.at[pl.ds(base, over)], dst_ref=tl.at[pl.ds(leaf * over, over)], send_sem=st.at[0],
            recv_sem=st.at[1], device_id=pair_id, device_id_type=MESH)

    tail_here = pltpu.make_async_copy(pu.at[pl.ds(base, over)], tl.at[pl.ds(mine * over, over)], lo.at[2]) if over else None
    own_here = pltpu.make_async_copy(pu.at[pl.ds(0, base + over)], g.at[pl.ds(own_at, base + over)], lo.at[0])
    half = hb * BLK
    fill = pltpu.make_async_copy(
        sep.at[:, pl.ds(pl.multiple_of(mine * half, half), half)],
        acc.at[pl.ds(0, nb * BLK), pl.ds(0, half)], lo.at[5])
    low_here = pltpu.make_async_copy(pc.at[nl], gc.at[low_slot(mine * n_col + c)], lo.at[1])

    def carry_copy(way, h, target):
        n = pl.ds(0, carry[h])
        return pltpu.make_async_remote_copy(
            src_ref=mo[way].at[n], dst_ref=mv[way].at[n], send_sem=sm.at[way], recv_sem=rm.at[way],
            device_id={"row": target}, device_id_type=MESH)

    def carry_at(way, h, leaf):
        start = n_row * 2 * full_u + (2 * carry_max if way == 0 else 0) + leaf * carry_max
        return g.at[pl.ds(start, carry[h])]

    def carry_hand(way, h, leaf):
        at = carry_at(way, h, leaf)
        return pltpu.make_async_remote_copy(
            src_ref=mv[way].at[pl.ds(0, carry[h])] if leaf is mine else at, dst_ref=at, send_sem=sd.at[way],
            recv_sem=rd.at[way], device_id=pair_id, device_id_type=MESH)

    def carry_here(way, h):
        return pltpu.make_async_copy(mv[way].at[pl.ds(0, carry[h])], carry_at(way, h, mine), lo.at[3 + way])

    def next_row(way):
        return r - 1 if way == 0 else r + 1

    def merge(way, h):
        t0, t1 = meta[1], meta[2]
        n_here = (t0 + t1 + 1 - mine) // 2

        @pl.loop(0, carry[h])
        def _(i):
            e = 2 * i + mine
            own = tl[jnp.clip(jnp.where(e < t0, e, over + e - t0), 0, 2 * over - 1)]
            if h > 0:
                prev = mv[way][jnp.clip(i - n_here, 0, carry[h - 1] - 1)]
                own = jnp.where(i < n_here, own, prev)
            mo[way][i] = own

    def at_hop(way, h):
        return n_row - 1 - h if way == 0 else h

    if over:
        tail(mine).start()
        tail_here.start()
    for part in range(PARTS):
        for way in range(2):
            line_send(way, 0, part, lambda copy: copy.start())
    for d in range(1, n_col):
        across(d, mine * n_col + c).start()
    pair(0, mine).start()
    hand_own(mine).start()
    own_here.start()
    fill.start()
    low_here.start()
    if over:
        tail(1 - mine).wait_recv()
        tail_here.wait()
        for way in range(2):
            @pl.when(r == at_hop(way, 0))
            def _(way=way):
                merge(way, 0)
                carry_copy(way, 0, next_row(way)).start()
    gather_tables(n_row, n_col, tr, tc, hb, nb, base, full_u, full_l, carry_max, named_u, named_l, tab)
    for step in range(n_row - 1):
        for part in range(PARTS):
            for way in range(2):
                line_wait(way, step, part)
                if step < n_row - 2:
                    line_send(way, step + 1, part, lambda copy: copy.start())
                hand_if(way, step, part, mine, lambda copy: copy.start())
        if over:
            for way in range(2):
                @pl.when(r == at_hop(way, step + 1))
                def _(way=way):
                    carry_copy(way, step, next_row(1 - way)).wait_recv()
                    if step < n_row - 2:
                        merge(way, step + 1)
                    carry_hand(way, step, mine).start()
                    carry_here(way, step).start()
                    if step < n_row - 2:
                        carry_copy(way, step + 1, next_row(way)).start()
        if step == 0:
            for d in range(1, n_col):
                across(d, from_slot(d, mine)).wait_recv()
                pair(d, mine).start()
    for d in range(n_col):
        pair(d, 1 - mine).wait_recv()
    hand_own(1 - mine).wait_recv()
    for step in range(n_row - 1):
        for part in range(PARTS):
            for way in range(2):
                hand_if(way, step, part, 1 - mine, lambda copy: copy.wait_recv())
    if over:
        for step in range(n_row - 1):
            for way in range(2):
                @pl.when(r == at_hop(way, step + 1))
                def _(way=way):
                    carry_hand(way, step, 1 - mine).wait_recv()
                    carry_hand(way, step, mine).wait_send()
                    carry_here(way, step).wait()

                @pl.when(r == at_hop(way, step))
                def _(way=way):
                    carry_copy(way, step, next_row(way)).wait_send()
        tail(mine).wait_send()
    own_here.wait()
    fill.wait()
    low_here.wait()
    hand_own(mine).wait_send()
    for d in range(n_col):
        pair(d, mine).wait_send()
    for d in range(1, n_col):
        across(d, mine * n_col + c).wait_send()
    for step in range(n_row - 1):
        for part in range(PARTS):
            for way in range(2):
                line_send(way, step, part, lambda copy: copy.wait_send())
                hand_if(way, step, part, mine, lambda copy: copy.wait_send())


def split(x):
    hi = x.astype(jnp.bfloat16)
    return hi, (x - hi.astype(jnp.float32)).astype(jnp.bfloat16)


GROUP = 4


def solve_kernel(n_row, n_col, hb, nb, kk, full_l, tab, inv, g, gc, acc, out, _, low, up, stage, sem, out_sem):
    sw = W // BLK
    half, loc_rows = hb * BLK, nb * BLK
    rows_of = 2 * LEAFROWS
    row_tab = (1 + sw) * rows_of

    def row_of(m):
        return m // kk * LEAFROWS + lax.rem(m, kk)

    @pl.loop(0, 2 * kk)
    def _(m):
        at_m = row_of(m)

        @pl.loop(0, tab[at_m, BLK // 2])
        def _(n):
            at = pl.ds(pl.multiple_of(n * BLK, BLK), BLK)
            for q in range(sw):
                src = g.at[tab[(1 + q) * rows_of + at_m, n]]
                pltpu.make_async_copy(src, up.at[m, pl.ds(q * BLK, BLK), at], sem.at[m]).start()

        @pl.loop(0, tab[row_tab + at_m, BLK // 2])
        def _(n):
            at = pl.ds(pl.multiple_of(n * BLK, BLK), BLK)
            for q in range(sw):
                src = gc.at[tab[row_tab + (1 + q) * rows_of + at_m, n]]
                pltpu.make_async_copy(src, low.at[m, at, pl.ds(q * BLK, BLK)], sem.at[m]).start()

    wide = GROUP * BLK

    @pl.loop(0, 2 * kk)
    def _(m):
        at_m = row_of(m)
        n_u, n_l = tab[at_m, BLK // 2], tab[row_tab + at_m, BLK // 2]

        @pl.loop(0, (n_u + n_l) * sw)
        def _(n):
            pltpu.make_async_copy(g.at[0], low.at[m, pl.ds(0, BLK), pl.ds(0, BLK)], sem.at[m]).wait()

        @pl.loop(0, (n_l + GROUP - 1) // GROUP)
        def _(x):
            rows = pl.ds(pl.multiple_of(x * wide, wide), wide)

            @pl.loop(0, (n_u + GROUP - 1) // GROUP)
            def _(y):
                cols = pl.ds(pl.multiple_of(y * wide, wide), wide)
                prod = jnp.dot(low[m, rows, :], up[m, :, cols], preferred_element_type=jnp.float32)
                for i in range(GROUP):
                    row = tab[row_tab + at_m, x * GROUP + i]
                    to = pl.ds(pl.multiple_of(row * BLK, BLK), BLK)
                    for j in range(GROUP):
                        col = tab[at_m, y * GROUP + j]
                        at = pl.ds(pl.multiple_of(col * BLK, BLK), BLK)
                        acc[to, at] -= prod[i * BLK:(i + 1) * BLK, j * BLK:(j + 1) * BLK]

    tile = min(512, half)
    steps = loc_rows // W

    def put(b, slot):
        return pltpu.make_async_copy(stage.at[slot], out.at[pl.ds(pl.multiple_of(b * W, W), W)], out_sem.at[slot])

    @pl.loop(0, steps)
    def _(b):
        slot = lax.rem(b, 2)

        @pl.when(b >= 2)
        def _():
            put(b - 2, slot).wait()

        rows = pl.ds(pl.multiple_of(b * W, W), W)
        f_hi, f_lo = split(inv[rows, :])
        for n in range(half // tile):
            at = pl.ds(n * tile, tile)
            hi, lo = split(acc[rows, at])
            stage[slot, :, at] = (jnp.dot(f_hi, hi, preferred_element_type=jnp.float32)
                                  + (jnp.dot(f_hi, lo, preferred_element_type=jnp.float32)
                                     + jnp.dot(f_lo, hi, preferred_element_type=jnp.float32)))
        put(b, slot).start()

    for b in range(max(0, steps - 2), steps):
        put(b, b % 2).wait()


def solve_call(n_row, n_col, hb, nb, kk, full_l):
    hbm = pl.BlockSpec(memory_space=pl.ANY)
    half, loc_rows = hb * BLK, nb * BLK
    hg, ng = -(-hb // GROUP) * GROUP, -(-nb // GROUP) * GROUP
    vmem = pl.BlockSpec(memory_space=pltpu.VMEM)
    acc = pltpu.VMEM((loc_rows + BLK, half + BLK), jnp.float32)

    def run(tab, *args):
        return pl.pallas_call(
            functools.partial(solve_kernel, n_row, n_col, hb, nb, kk, full_l),
            out_shape=(jax.ShapeDtypeStruct((loc_rows, half), jnp.float32), acc),
            in_specs=[pl.BlockSpec(memory_space=pltpu.SMEM), vmem, hbm, hbm, vmem], out_specs=(hbm, vmem),
            scratch_shapes=[pltpu.VMEM((2 * kk, ng * BLK, W), jnp.bfloat16),
                            pltpu.VMEM((2 * kk, W, hg * BLK), jnp.bfloat16),
                            pltpu.VMEM((2, W, half), jnp.float32),
                            pltpu.SemaphoreType.DMA((2 * kk,)), pltpu.SemaphoreType.DMA((2,))],
            input_output_aliases={4: 1},
            compiler_params=pltpu.CompilerParams(vmem_limit_bytes=40 * 2**20),
            name="solve",
        )(tab, *args)[0]
    return run


def kinds_of(full_u, full_l, n_row):
    base, over = -(-full_u * 20 // 96), -(-full_u * 24 // 96)
    found = []
    for last, inner, first, low in ((12, 12, 12, 22), (14, 14, 14, 24), (15, 15, 14, 24), (16, 16, 14, 24), (17, 16, 14, 24),
                                    (19, 17, 15, 26), (22, 19, 16, 26), (32, 28, 20, 28)):
        sizes = [first] + [inner] * (n_row - 3) + [last]
        found.append((base, over, tuple(-(-full_u * v // 96) for v in sizes[:n_row - 1]), -(-full_l * low // 48)))
    found.append((-(-full_u * 48 // 96), 0, None, -(-full_l * 40 // 48)))
    found.append((full_u, 0, None, full_l))
    return found


def sparse_device(n_row, n_col, separator, col_panels, row_panels, rows_list, cols_list, inverses):
    loc_rows, loc_cols = separator.shape
    half = loc_cols // 2
    tr, tc = row_panels.shape[1] // BLK, col_panels.shape[2] // BLK
    hb, nb = half // BLK, loc_rows // BLK
    kk = rows_list.shape[1]
    sw = W // BLK
    full_u, full_l = 2 * tr * hb, tc * nb
    kinds = kinds_of(full_u, full_l, n_row)
    carry_max = max(max(kind[2]) for kind in kinds if kind[2])
    over = kinds[0][1]

    block = (BLK, BLK)
    bf16 = jnp.bfloat16
    hbm = pl.BlockSpec(memory_space=pl.ANY)
    vmem = pl.BlockSpec(memory_space=pltpu.VMEM)
    smem = pl.BlockSpec(memory_space=pltpu.SMEM)
    dma = pltpu.SemaphoreType.DMA
    n_ku, n_kl = -(-tr // sw) + 1, -(-tc // sw) + 1
    named = (2 * LEAFROWS, BLK)
    pu, pc, meta, named_u, named_l = pl.pallas_call(
        functools.partial(pack_kernel, n_row, n_col, tr, tc, hb, nb, kk, kinds),
        out_shape=(jax.ShapeDtypeStruct((full_u,) + block, bf16), jax.ShapeDtypeStruct((full_l,) + block, bf16),
                   jax.ShapeDtypeStruct((3,), jnp.int32), jax.ShapeDtypeStruct(named, jnp.float32),
                   jax.ShapeDtypeStruct(named, jnp.float32)),
        in_specs=[smem, smem, hbm, hbm], out_specs=(hbm, hbm, smem, vmem, vmem),
        scratch_shapes=[pltpu.SMEM((n_ku * (2 * hb + 1),), jnp.int32), pltpu.SMEM((n_kl * (nb + 1),), jnp.int32),
                        pltpu.VMEM((full_u,) + block, bf16), pltpu.VMEM((full_l,) + block, bf16), dma, dma],
        compiler_params=pltpu.CompilerParams(vmem_limit_bytes=60 * 2**20),
        name="pack",
    )(cols_list, rows_list, row_panels, col_panels)

    n_all = n_row * 2 * full_u + 4 * carry_max
    tab_rows = 2 * (1 + sw) * 2 * LEAFROWS

    def exchange(which):
        def run(meta, named_u, named_l, pu, pc, separator, inverses):
            g, gc, tab, acc = pl.pallas_call(
                functools.partial(comm_kernel, n_row, n_col, tr, tc, hb, nb, full_u, full_l, carry_max, kinds[which]),
                out_shape=(jax.ShapeDtypeStruct((n_all,) + block, bf16),
                           jax.ShapeDtypeStruct((2 * n_col * full_l,) + block, bf16),
                           jax.ShapeDtypeStruct((tab_rows, BLK), jnp.int32),
                           pltpu.VMEM((loc_rows + BLK, half + BLK), jnp.float32)),
                in_specs=[smem, vmem, vmem, hbm, hbm, hbm], out_specs=(hbm, hbm, vmem, vmem),
                scratch_shapes=[pltpu.VMEM((2 * over,) + block, bf16),
                                *[pltpu.VMEM((carry_max,) + block, bf16)] * 4]
                + [dma((2, n_row, PARTS))] * 4 + [dma((n_col,))] * 4 + [dma((2,))] * 7 + [dma((6,))],
                compiler_params=pltpu.CompilerParams(collective_id=which, has_side_effects=True,
                                                     vmem_limit_bytes=40 * 2**20),
                name="exchange%d" % which,
            )(meta, named_u, named_l, pu, pc, separator)
            return solve_call(n_row, n_col, hb, nb, kk, full_l)(tab, inverses, g, gc, acc)
        return run

    return lax.switch(meta[0], [exchange(i) for i in range(len(kinds))],
                      meta, named_u, named_l, pu, pc, separator, inverses)


def solution(mesh):
    placed = (
        P("row", "col"),
        P("leaf", "row", "col"),
        P("leaf", "row", "col"),
        P(),
        P(),
        P("row", None),
    )
    n_row, n_col = mesh.shape["row"], mesh.shape["col"]

    def per_device(separator, col_panels, row_panels, *rest):
        whole = separator.shape[1] % (2 * W) == 0 and separator.shape[0] % W == 0
        fits = (rest[0].shape[1] <= LEAFROWS and 3 <= n_row <= LEAFROWS and n_col <= LEAFROWS
                and n_row * separator.shape[0] <= BLK * BLK and n_col * separator.shape[1] <= BLK * BLK)
        if whole and row_panels.shape[1] % BLK == 0 and col_panels.shape[2] % BLK == 0 and mesh.shape["leaf"] == 2 and fits:
            return sparse_device(n_row, n_col, separator, col_panels, row_panels, *rest)
        return dense_device(separator, col_panels, row_panels, *rest)

    return jax.shard_map(
        per_device, mesh=mesh, in_specs=placed, out_specs=P("row", ("col", "leaf")), check_vma=False
    )
```

```python
import functools

import jax
import jax.numpy as jnp
from jax import lax
from jax.experimental import pallas as pl
from jax.experimental.pallas import tpu as pltpu
from jax.sharding import PartitionSpec as P

W = 256
BLK = 128
MESH = pl.DeviceIdType.MESH
PARTS = 2
LEAFROWS = 8


def touched(index_list, positions):
    return jnp.any(index_list[:, :, :, None] == (positions // BLK)[None, None, None, :], axis=2)


def dense_device(separator, col_panels, row_panels, rows_list, cols_list, inverses):
    loc_rows = separator.shape[0]
    loc_cols = separator.shape[1]
    half = loc_cols // 2
    mine = lax.axis_index("leaf")
    row_ids = lax.axis_index("row") * loc_rows + jnp.arange(loc_rows, dtype=jnp.int32)
    subtrees = jnp.stack([mine])
    col_ids = lax.axis_index("col") * loc_cols + jnp.arange(loc_cols, dtype=jnp.int32)
    row_mask = touched(jnp.take(rows_list, subtrees, axis=0), row_ids)
    col_mask = touched(jnp.take(cols_list, subtrees, axis=0), col_ids)
    upper_all = lax.all_gather(row_panels, "row", axis=1, tiled=True)
    owner_all = jnp.arange(upper_all.shape[1], dtype=jnp.int32) // W
    keep_upper = jnp.take(col_mask, owner_all, axis=1)
    upper_all = jnp.where(keep_upper, upper_all, jnp.zeros_like(upper_all))
    piece = lax.all_gather(col_panels, "col", axis=2, tiled=True)
    owner = jnp.arange(piece.shape[2], dtype=jnp.int32) // W
    keep_lower = jnp.transpose(jnp.take(row_mask, owner, axis=1), (0, 2, 1))
    masked = jnp.where(keep_lower, piece, jnp.zeros_like(piece))
    update = jnp.einsum("srj,sjc->rc", masked, upper_all, preferred_element_type=jnp.float32)
    own_part = lax.dynamic_slice_in_dim(separator, mine * half, half, 1)
    both = lax.psum_scatter(update, "leaf", scatter_dimension=1, tiled=True)
    combined = own_part - both
    blocks = combined.reshape(loc_rows // W, W, half)
    factor = inverses.reshape(loc_rows // W, W, W)
    solved = jnp.einsum("bij,bjc->bic", factor, blocks, precision=lax.Precision.HIGHEST)
    return solved.reshape(loc_rows, half)


def mm(a, b):
    return jnp.dot(a.astype(jnp.bfloat16), b.astype(jnp.bfloat16), preferred_element_type=jnp.float32)


def grid_ids(shape):
    return lax.broadcasted_iota(jnp.int32, shape, 0), lax.broadcasted_iota(jnp.int32, shape, 1)


def ones_where(mask):
    return jnp.where(mask, jnp.float32(1), jnp.float32(0))


def list_mask(lists, leaves, kk, held):
    width = lists.shape[0] // (leaves * kk)
    lane = lax.broadcasted_iota(jnp.int32, (1, BLK), 1)
    held[...] = jnp.zeros(held.shape, jnp.float32)
    for leaf in range(leaves):
        for k in range(kk):
            at = (leaf * kk + k) * width
            hit = lane == lists[at]
            for e in range(1, width):
                hit = jnp.logical_or(hit, lane == lists[at + e])
            held[leaf * LEAFROWS + k:leaf * LEAFROWS + k + 1, :] = ones_where(hit)
    return held[...]


def slice_counts(tr, sw, n_own):
    y, m = grid_ids((2 * LEAFROWS, 2 * LEAFROWS))
    same = jnp.logical_and(y // LEAFROWS == m // LEAFROWS, y % LEAFROWS < n_own)
    total = jnp.zeros(y.shape, jnp.float32)
    for t in range(tr):
        s = (y % LEAFROWS) * tr + t
        first = (m % LEAFROWS) * sw
        total = total + ones_where(same & (s >= first) & (s < first + sw))
    return total


def core_tails(counts, base):
    y, m = grid_ids((2 * LEAFROWS, 2 * LEAFROWS))
    past = jnp.maximum(counts - base, 0.0)
    chip = mm(ones_where(y % LEAFROWS == m % LEAFROWS), past)
    core = lax.broadcasted_iota(jnp.int32, past.shape, 0) // LEAFROWS
    carried = jnp.floor((chip + 1.0 - core.astype(jnp.float32)) * 0.5)
    return past, carried


def pack_kernel(n_row, n_col, tr, tc, hb, nb, kk, kinds, cols_s, rows_s, upper, lower,
                pu, pc, meta, named_u, named_l, flag_u, flag_l, pu_v, pc_v, sem_in, sem_out):
    r, c, mine = lax.axis_index("row"), lax.axis_index("col"), lax.axis_index("leaf")
    sw = W // BLK
    wb = 2 * hb
    n_ku, n_kl = -(-tr // sw) + 1, -(-tc // sw) + 1
    width_u, width_l = cols_s.shape[0] // (2 * kk), rows_s.shape[0] // (2 * kk)
    first_u, first_l = r * tr // sw, c * tc // sw

    @pl.loop(0, n_ku * (wb + 1))
    def _(i):
        flag_u[i] = jnp.int32(0)

    @pl.loop(0, n_kl * (nb + 1))
    def _(i):
        flag_l[i] = jnp.int32(0)

    for q in range(n_ku):
        at = (mine * kk + jnp.minimum(first_u + q, kk - 1)) * width_u
        for e in range(width_u):
            v = cols_s[at + e] - c * wb
            flag_u[q * (wb + 1) + jnp.where((v >= 0) & (v < wb), v, wb)] = jnp.int32(1)
    for q in range(n_kl):
        at = (mine * kk + jnp.minimum(first_l + q, kk - 1)) * width_l
        for e in range(width_l):
            v = rows_s[at + e] - r * nb
            flag_l[q * (nb + 1) + jnp.where((v >= 0) & (v < nb), v, nb)] = jnp.int32(1)

    n_u = n_l = jnp.int32(0)
    for t in range(tr):
        flags = ((r * tr + t) // sw - first_u) * (wb + 1)

        def take_upper(j, n, t=t, flags=flags):
            hit = flag_u[flags + j]

            @pl.when(hit > 0)
            def _():
                src = upper.at[0, pl.ds(t * BLK, BLK), pl.ds(pl.multiple_of(j * BLK, BLK), BLK)]
                pltpu.make_async_copy(src, pu_v.at[n], sem_in).start()
            return n + hit

        n_u = lax.fori_loop(0, wb, take_upper, n_u)
    for t in range(tc):
        flags = ((c * tc + t) // sw - first_l) * (nb + 1)

        def take_lower(j, n, t=t, flags=flags):
            hit = flag_l[flags + j]

            @pl.when(hit > 0)
            def _():
                src = lower.at[0, pl.ds(pl.multiple_of(j * BLK, BLK), BLK), pl.ds(t * BLK, BLK)]
                pltpu.make_async_copy(src, pc_v.at[n], sem_in).start()
            return n + hit

        n_l = lax.fori_loop(0, nb, take_lower, n_l)

    row, lane = grid_ids((2 * LEAFROWS, BLK))
    J, x = grid_ids((BLK, BLK))
    cnt = mm(list_mask(cols_s, 2, kk, named_u), ones_where((J >= x * wb) & (J < (x + 1) * wb)))
    counts = mm(slice_counts(tr, sw, n_row), cnt)
    cnt_l = mm(list_mask(rows_s, 2, kk, named_l), ones_where((J >= x * nb) & (J < (x + 1) * nb)))
    counts_l = mm(slice_counts(tc, sw, n_col), cnt_l)
    base = kinds[0][0]
    past, carried = core_tails(counts, base)
    y, m = grid_ids((2 * LEAFROWS, 2 * LEAFROWS))
    same = y // LEAFROWS == m // LEAFROWS
    hop, src = y % LEAFROWS, m % LEAFROWS
    live = same & (hop <= n_row - 2) & (src < n_row)
    most = jnp.maximum(mm(ones_where(live & (src <= hop)), carried),
                       mm(ones_where(live & (src >= n_row - 1 - hop)), carried))
    hops = [jnp.max(jnp.where(row % LEAFROWS == h, most, 0.0)).astype(jnp.int32) for h in range(n_row - 1)]
    most_past = jnp.max(past).astype(jnp.int32)
    most_u = jnp.max(counts).astype(jnp.int32)
    most_l = jnp.max(counts_l).astype(jnp.int32)
    level = jnp.int32(0)
    for cap, over, carry, cap_l in kinds[:-1]:
        bad = most_l > cap_l
        if over:
            bad = jnp.logical_or(bad, most_past > over)
            for h in range(n_row - 1):
                bad = jnp.logical_or(bad, hops[h] > carry[h])
        else:
            bad = jnp.logical_or(bad, most_u > cap)
        level = level + bad.astype(jnp.int32)
    meta[0] = level
    for leaf in range(2):
        meta[1 + leaf] = jnp.sum(jnp.where((row == leaf * LEAFROWS + r) & (lane == c), past, 0.0)).astype(jnp.int32)

    @pl.loop(0, n_u + n_l)
    def _(i):
        pltpu.make_async_copy(pu.at[0], pu_v.at[0], sem_in).wait()

    step = 8

    def put(i, full, src, dst):
        at = pl.ds(jnp.minimum(i * step, full - step), step)
        return pltpu.make_async_copy(src.at[at], dst.at[at], sem_out)

    @pl.loop(0, (n_u + step - 1) // step)
    def _(i):
        put(i, pu.shape[0], pu_v, pu).start()

    @pl.loop(0, (n_l + step - 1) // step)
    def _(i):
        put(i, pc.shape[0], pc_v, pc).start()

    @pl.loop(0, (n_u + step - 1) // step + (n_l + step - 1) // step)
    def _(i):
        put(0, pu.shape[0], pu_v, pu).wait()


def gather_tables(n_row, n_col, tr, tc, hb, nb, base, full_u, full_l, carry_max, named_u, named_l, tab):
    r, c, mine = lax.axis_index("row"), lax.axis_index("col"), lax.axis_index("leaf")
    sw, wb = W // BLK, 2 * hb
    rows = 2 * LEAFROWS
    row, lane = grid_ids((rows, BLK))
    J, x = grid_ids((BLK, BLK))
    y, m = grid_ids((rows, rows))
    leaf, k = row // LEAFROWS, row % LEAFROWS
    before = ones_where(J < x)
    every = jnp.ones((BLK, BLK), jnp.float32)

    def pick(start, count):
        return ones_where((J == start + x) & (x < count))

    def slices(q, per, n_own):
        s = k * sw + q
        owner = jnp.zeros(s.shape, jnp.int32)
        for o in range(1, n_own):
            owner = owner + (s >= o * per).astype(jnp.int32)
        s_y = (y % LEAFROWS) * sw + q
        own_y = jnp.zeros(y.shape, jnp.int32)
        for o in range(1, n_own):
            own_y = own_y + (s_y >= o * per).astype(jnp.int32)
        weight = jnp.zeros(y.shape, jnp.float32)
        for other in range(sw):
            s_m = (m % LEAFROWS) * sw + other
            weight = weight + ones_where((y // LEAFROWS == m // LEAFROWS) & (s_m >= own_y * per) & (s_m < s_y))
        return owner, own_y, weight

    def store(mask, locs, n, at):
        rank = mm(mask, before)
        count = mm(mask, every)
        outs = [jnp.full(mask.shape, float(n), jnp.float32)] + [jnp.zeros(mask.shape, jnp.float32) for _ in locs]
        for i in range(n):
            sel = (mask > 0) & (rank == float(i))
            vals = [lane.astype(jnp.float32)] + locs
            for o in range(len(outs)):
                got = jnp.sum(jnp.where(sel, vals[o], 0.0), axis=1, keepdims=True)
                outs[o] = jnp.where((lane == i) & (count > float(i)), got, outs[o])
        outs[0] = jnp.where(lane == BLK // 2, count, outs[0])
        for o, v in enumerate(outs):
            tab[(at + o) * rows:(at + o + 1) * rows, :] = v.astype(jnp.int32)

    mask = named_u[...]
    chip = mm(mask, pick(c * wb, wb))
    cnt = mm(chip, every)
    rank = mm(chip, before)
    past, carried = core_tails(mm(slice_counts(tr, sw, n_row), cnt), base)
    half = pick(mine * hb, hb)
    mask_h, rank_h = mm(chip, half), mm(rank, half)
    locs = []
    for q in range(sw):
        owner, own_y, weight = slices(q, tr, n_row)
        p = mm(weight, cnt) + rank_h
        mine_y = m % LEAFROWS
        added = mm(ones_where((y // LEAFROWS == 1) & (m // LEAFROWS == 0) & (mine_y == own_y)), past)
        inner = ((own_y < mine_y) & (mine_y < r)) | ((r < mine_y) & (mine_y < own_y))
        passed = [mm(ones_where((m // LEAFROWS == a) & inner & (mine_y < n_row)), carried) for a in range(2)]
        e = p - base + added
        e_half = jnp.floor(e * 0.5)
        odd = e - 2.0 * e_half > 0.5
        plain = (owner * 2 + leaf).astype(jnp.float32) * full_u + p
        region = jnp.where(owner < r, n_row * 2 * full_u, n_row * 2 * full_u + 2 * carry_max).astype(jnp.float32)
        far = region + e_half + jnp.where(odd, passed[1] + carry_max, passed[0])
        locs.append(jnp.where((p < base) | (owner == r), plain, far))
    store(mask_h, locs, hb, 0)

    mask = named_l[...]
    mine_l = mm(mask, pick(r * nb, nb))
    cnt = mm(mine_l, every)
    rank = mm(mine_l, before)
    locs = []
    for q in range(sw):
        owner, _, weight = slices(q, tc, n_col)
        locs.append((leaf * n_col + owner).astype(jnp.float32) * full_l + mm(weight, cnt) + rank)
    store(mine_l, locs, nb, 1 + sw)


def comm_kernel(n_row, n_col, tr, tc, hb, nb, full_u, full_l, carry_max, kind,
                meta, named_u, named_l, pu, pc, sep, g, gc, tab, acc,
                tl, mv0, mv1, mo0, mo1, su, ru, sb, rb, sl, rl, sf, rf, sm, rm, sd, rd, so, st, rt, lo):
    base, over, carry, cap_l = kind
    mv, mo = (mv0, mv1), (mo0, mo1)
    r, c, mine = lax.axis_index("row"), lax.axis_index("col"), lax.axis_index("leaf")
    nl = pl.ds(0, cap_l)

    def low_slot(slot):
        return pl.ds(slot * full_l, cap_l)

    barrier = pltpu.get_barrier_semaphore()
    for d in (1, n_row - 1):
        pl.semaphore_signal(barrier, inc=1, device_id={"row": lax.rem(r + d, n_row)}, device_id_type=MESH)
    for d in range(1, n_col):
        pl.semaphore_signal(barrier, inc=1, device_id={"col": lax.rem(c + d, n_col)}, device_id_type=MESH)
    pl.semaphore_signal(barrier, inc=1, device_id={"leaf": 1 - mine}, device_id_type=MESH)
    pl.semaphore_wait(barrier, n_col + 2)

    cuts = [base * x // PARTS for x in range(PARTS + 1)]
    own_at = (r * 2 + mine) * full_u
    pair_id = {"leaf": 1 - mine}

    def blocks(shard, part, leaf):
        return g.at[pl.ds((shard * 2 + leaf) * full_u + cuts[part], cuts[part + 1] - cuts[part])]

    def line(way, step, part, shard, target):
        src = pu.at[pl.ds(cuts[part], cuts[part + 1] - cuts[part])] if step == 0 else blocks(shard, part, mine)
        return pltpu.make_async_remote_copy(
            src_ref=src, dst_ref=blocks(shard, part, mine), send_sem=su.at[way, step, part],
            recv_sem=ru.at[way, step, part], device_id={"row": target}, device_id_type=MESH)

    def line_send(way, step, part, act):
        goes = jnp.logical_and(r >= 1, r + step <= n_row - 1) if way == 0 else jnp.logical_and(r <= n_row - 2, r >= step)

        @pl.when(goes)
        def _():
            act(line(way, step, part, r + step if way == 0 else r - step, r - 1 if way == 0 else r + 1))

    def came(way, step):
        return r + 1 + step <= n_row - 1 if way == 0 else r >= 1 + step

    def shard_of(way, step):
        return r + 1 + step if way == 0 else r - 1 - step

    def line_wait(way, step, part):
        @pl.when(came(way, step))
        def _():
            line(way, step, part, shard_of(way, step), r + 1 if way == 0 else r - 1).wait_recv()

    def hand(way, step, part, leaf):
        at = blocks(shard_of(way, step), part, leaf)
        return pltpu.make_async_remote_copy(
            src_ref=at, dst_ref=at, send_sem=sb.at[way, step, part], recv_sem=rb.at[way, step, part],
            device_id=pair_id, device_id_type=MESH)

    def hand_if(way, step, part, leaf, act):
        @pl.when(came(way, step))
        def _():
            act(hand(way, step, part, leaf))

    def hand_own(leaf):
        at = g.at[pl.ds((r * 2 + leaf) * full_u, base + over)]
        return pltpu.make_async_remote_copy(
            src_ref=pu.at[pl.ds(0, base + over)] if leaf is mine else at, dst_ref=at, send_sem=so.at[0],
            recv_sem=so.at[1], device_id=pair_id, device_id_type=MESH)

    def across(d, slot):
        return pltpu.make_async_remote_copy(
            src_ref=pc.at[nl], dst_ref=gc.at[low_slot(slot)], send_sem=sl.at[d], recv_sem=rl.at[d],
            device_id={"col": lax.rem(c + d, n_col)}, device_id_type=MESH)

    def from_slot(d, leaf):
        return leaf * n_col + lax.rem(c + n_col - d, n_col)

    def pair(d, leaf):
        slot = from_slot(d, leaf)
        return pltpu.make_async_remote_copy(
            src_ref=pc.at[nl] if d == 0 else gc.at[low_slot(slot)], dst_ref=gc.at[low_slot(slot)],
            send_sem=sf.at[d], recv_sem=rf.at[d], device_id=pair_id, device_id_type=MESH)

    def tail(leaf):
        return pltpu.make_async_remote_copy(
            src_ref=pu.at[pl.ds(base, over)], dst_ref=tl.at[pl.ds(leaf * over, over)], send_sem=st.at[0],
            recv_sem=st.at[1], device_id=pair_id, device_id_type=MESH)

    tail_here = pltpu.make_async_copy(pu.at[pl.ds(base, over)], tl.at[pl.ds(mine * over, over)], lo.at[2]) if over else None
    own_here = pltpu.make_async_copy(pu.at[pl.ds(0, base + over)], g.at[pl.ds(own_at, base + over)], lo.at[0])
    half = hb * BLK
    fill = pltpu.make_async_copy(
        sep.at[:, pl.ds(pl.multiple_of(mine * half, half), half)],
        acc.at[pl.ds(0, nb * BLK), pl.ds(0, half)], lo.at[5])
    low_here = pltpu.make_async_copy(pc.at[nl], gc.at[low_slot(mine * n_col + c)], lo.at[1])

    def carry_copy(way, h, target):
        n = pl.ds(0, carry[h])
        return pltpu.make_async_remote_copy(
            src_ref=mo[way].at[n], dst_ref=mv[way].at[n], send_sem=sm.at[way], recv_sem=rm.at[way],
            device_id={"row": target}, device_id_type=MESH)

    def carry_at(way, h, leaf):
        start = n_row * 2 * full_u + (2 * carry_max if way == 0 else 0) + leaf * carry_max
        return g.at[pl.ds(start, carry[h])]

    def carry_hand(way, h, leaf):
        at = carry_at(way, h, leaf)
        return pltpu.make_async_remote_copy(
            src_ref=mv[way].at[pl.ds(0, carry[h])] if leaf is mine else at, dst_ref=at, send_sem=sd.at[way],
            recv_sem=rd.at[way], device_id=pair_id, device_id_type=MESH)

    def carry_here(way, h):
        return pltpu.make_async_copy(mv[way].at[pl.ds(0, carry[h])], carry_at(way, h, mine), lo.at[3 + way])

    def next_row(way):
        return r - 1 if way == 0 else r + 1

    def merge(way, h):
        t0, t1 = meta[1], meta[2]
        n_here = (t0 + t1 + 1 - mine) // 2

        @pl.loop(0, carry[h])
        def _(i):
            e = 2 * i + mine
            own = tl[jnp.clip(jnp.where(e < t0, e, over + e - t0), 0, 2 * over - 1)]
            if h > 0:
                prev = mv[way][jnp.clip(i - n_here, 0, carry[h - 1] - 1)]
                own = jnp.where(i < n_here, own, prev)
            mo[way][i] = own

    def at_hop(way, h):
        return n_row - 1 - h if way == 0 else h

    if over:
        tail(mine).start()
        tail_here.start()
    for part in range(PARTS):
        for way in range(2):
            line_send(way, 0, part, lambda copy: copy.start())
    for d in range(1, n_col):
        across(d, mine * n_col + c).start()
    pair(0, mine).start()
    hand_own(mine).start()
    own_here.start()
    fill.start()
    low_here.start()
    if over:
        tail(1 - mine).wait_recv()
        tail_here.wait()
        for way in range(2):
            @pl.when(r == at_hop(way, 0))
            def _(way=way):
                merge(way, 0)
                carry_copy(way, 0, next_row(way)).start()
    gather_tables(n_row, n_col, tr, tc, hb, nb, base, full_u, full_l, carry_max, named_u, named_l, tab)
    for step in range(n_row - 1):
        for part in range(PARTS):
            for way in range(2):
                line_wait(way, step, part)
                if step < n_row - 2:
                    line_send(way, step + 1, part, lambda copy: copy.start())
                hand_if(way, step, part, mine, lambda copy: copy.start())
        if over:
            for way in range(2):
                @pl.when(r == at_hop(way, step + 1))
                def _(way=way):
                    carry_copy(way, step, next_row(1 - way)).wait_recv()
                    if step < n_row - 2:
                        merge(way, step + 1)
                    carry_hand(way, step, mine).start()
                    carry_here(way, step).start()
                    if step < n_row - 2:
                        carry_copy(way, step + 1, next_row(way)).start()
        if step == 1:
            for d in range(1, n_col):
                across(d, from_slot(d, mine)).wait_recv()
                pair(d, mine).start()
    for d in range(n_col):
        pair(d, 1 - mine).wait_recv()
    hand_own(1 - mine).wait_recv()
    for step in range(n_row - 1):
        for part in range(PARTS):
            for way in range(2):
                hand_if(way, step, part, 1 - mine, lambda copy: copy.wait_recv())
    if over:
        for step in range(n_row - 1):
            for way in range(2):
                @pl.when(r == at_hop(way, step + 1))
                def _(way=way):
                    carry_hand(way, step, 1 - mine).wait_recv()
                    carry_hand(way, step, mine).wait_send()
                    carry_here(way, step).wait()

                @pl.when(r == at_hop(way, step))
                def _(way=way):
                    carry_copy(way, step, next_row(way)).wait_send()
        tail(mine).wait_send()
    own_here.wait()
    fill.wait()
    low_here.wait()
    hand_own(mine).wait_send()
    for d in range(n_col):
        pair(d, mine).wait_send()
    for d in range(1, n_col):
        across(d, mine * n_col + c).wait_send()
    for step in range(n_row - 1):
        for part in range(PARTS):
            for way in range(2):
                line_send(way, step, part, lambda copy: copy.wait_send())
                hand_if(way, step, part, mine, lambda copy: copy.wait_send())


def split(x):
    hi = x.astype(jnp.bfloat16)
    return hi, (x - hi.astype(jnp.float32)).astype(jnp.bfloat16)


GROUP = 4


def solve_kernel(n_row, n_col, hb, nb, kk, full_l, tab, inv, g, gc, acc, out, _, low, up, stage, sem, out_sem):
    sw = W // BLK
    half, loc_rows = hb * BLK, nb * BLK
    rows_of = 2 * LEAFROWS
    row_tab = (1 + sw) * rows_of

    def row_of(m):
        return m // kk * LEAFROWS + lax.rem(m, kk)

    @pl.loop(0, 2 * kk)
    def _(m):
        at_m = row_of(m)

        @pl.loop(0, tab[at_m, BLK // 2])
        def _(n):
            at = pl.ds(pl.multiple_of(n * BLK, BLK), BLK)
            for q in range(sw):
                src = g.at[tab[(1 + q) * rows_of + at_m, n]]
                pltpu.make_async_copy(src, up.at[m, pl.ds(q * BLK, BLK), at], sem.at[m]).start()

        @pl.loop(0, tab[row_tab + at_m, BLK // 2])
        def _(n):
            at = pl.ds(pl.multiple_of(n * BLK, BLK), BLK)
            for q in range(sw):
                src = gc.at[tab[row_tab + (1 + q) * rows_of + at_m, n]]
                pltpu.make_async_copy(src, low.at[m, at, pl.ds(q * BLK, BLK)], sem.at[m]).start()

    wide = GROUP * BLK

    @pl.loop(0, 2 * kk)
    def _(m):
        at_m = row_of(m)
        n_u, n_l = tab[at_m, BLK // 2], tab[row_tab + at_m, BLK // 2]

        @pl.loop(0, (n_u + n_l) * sw)
        def _(n):
            pltpu.make_async_copy(g.at[0], low.at[m, pl.ds(0, BLK), pl.ds(0, BLK)], sem.at[m]).wait()

        @pl.loop(0, (n_l + GROUP - 1) // GROUP)
        def _(x):
            rows = pl.ds(pl.multiple_of(x * wide, wide), wide)

            @pl.loop(0, (n_u + GROUP - 1) // GROUP)
            def _(y):
                cols = pl.ds(pl.multiple_of(y * wide, wide), wide)
                prod = jnp.dot(low[m, rows, :], up[m, :, cols], preferred_element_type=jnp.float32)
                for i in range(GROUP):
                    row = tab[row_tab + at_m, x * GROUP + i]
                    to = pl.ds(pl.multiple_of(row * BLK, BLK), BLK)
                    for j in range(GROUP):
                        col = tab[at_m, y * GROUP + j]
                        at = pl.ds(pl.multiple_of(col * BLK, BLK), BLK)
                        acc[to, at] -= prod[i * BLK:(i + 1) * BLK, j * BLK:(j + 1) * BLK]

    tile = min(512, half)
    steps = loc_rows // W

    def put(b, slot):
        return pltpu.make_async_copy(stage.at[slot], out.at[pl.ds(pl.multiple_of(b * W, W), W)], out_sem.at[slot])

    @pl.loop(0, steps)
    def _(b):
        slot = lax.rem(b, 2)

        @pl.when(b >= 2)
        def _():
            put(b - 2, slot).wait()

        rows = pl.ds(pl.multiple_of(b * W, W), W)
        f_hi, f_lo = split(inv[rows, :])
        for n in range(half // tile):
            at = pl.ds(n * tile, tile)
            hi, lo = split(acc[rows, at])
            stage[slot, :, at] = (jnp.dot(f_hi, hi, preferred_element_type=jnp.float32)
                                  + (jnp.dot(f_hi, lo, preferred_element_type=jnp.float32)
                                     + jnp.dot(f_lo, hi, preferred_element_type=jnp.float32)))
        put(b, slot).start()

    for b in range(max(0, steps - 2), steps):
        put(b, b % 2).wait()


def solve_call(n_row, n_col, hb, nb, kk, full_l):
    hbm = pl.BlockSpec(memory_space=pl.ANY)
    half, loc_rows = hb * BLK, nb * BLK
    hg, ng = -(-hb // GROUP) * GROUP, -(-nb // GROUP) * GROUP
    vmem = pl.BlockSpec(memory_space=pltpu.VMEM)
    acc = pltpu.VMEM((loc_rows + BLK, half + BLK), jnp.float32)

    def run(tab, *args):
        return pl.pallas_call(
            functools.partial(solve_kernel, n_row, n_col, hb, nb, kk, full_l),
            out_shape=(jax.ShapeDtypeStruct((loc_rows, half), jnp.float32), acc),
            in_specs=[pl.BlockSpec(memory_space=pltpu.SMEM), vmem, hbm, hbm, vmem], out_specs=(hbm, vmem),
            scratch_shapes=[pltpu.VMEM((2 * kk, ng * BLK, W), jnp.bfloat16),
                            pltpu.VMEM((2 * kk, W, hg * BLK), jnp.bfloat16),
                            pltpu.VMEM((2, W, half), jnp.float32),
                            pltpu.SemaphoreType.DMA((2 * kk,)), pltpu.SemaphoreType.DMA((2,))],
            input_output_aliases={4: 1},
            compiler_params=pltpu.CompilerParams(vmem_limit_bytes=40 * 2**20),
            name="solve",
        )(tab, *args)[0]
    return run


def kinds_of(full_u, full_l, n_row):
    base, over = -(-full_u * 20 // 96), -(-full_u * 24 // 96)
    found = []
    for last, inner, first, low in ((12, 12, 12, 22), (14, 14, 14, 24), (15, 15, 14, 24), (16, 16, 14, 24), (17, 16, 14, 24),
                                    (19, 17, 15, 26), (22, 19, 16, 26), (32, 28, 20, 28)):
        sizes = [first] + [inner] * (n_row - 3) + [last]
        found.append((base, over, tuple(-(-full_u * v // 96) for v in sizes[:n_row - 1]), -(-full_l * low // 48)))
    found.append((-(-full_u * 48 // 96), 0, None, -(-full_l * 40 // 48)))
    found.append((full_u, 0, None, full_l))
    return found


def sparse_device(n_row, n_col, separator, col_panels, row_panels, rows_list, cols_list, inverses):
    loc_rows, loc_cols = separator.shape
    half = loc_cols // 2
    tr, tc = row_panels.shape[1] // BLK, col_panels.shape[2] // BLK
    hb, nb = half // BLK, loc_rows // BLK
    kk = rows_list.shape[1]
    sw = W // BLK
    full_u, full_l = 2 * tr * hb, tc * nb
    kinds = kinds_of(full_u, full_l, n_row)
    carry_max = max(max(kind[2]) for kind in kinds if kind[2])
    over = kinds[0][1]

    block = (BLK, BLK)
    bf16 = jnp.bfloat16
    hbm = pl.BlockSpec(memory_space=pl.ANY)
    vmem = pl.BlockSpec(memory_space=pltpu.VMEM)
    smem = pl.BlockSpec(memory_space=pltpu.SMEM)
    dma = pltpu.SemaphoreType.DMA
    n_ku, n_kl = -(-tr // sw) + 1, -(-tc // sw) + 1
    named = (2 * LEAFROWS, BLK)
    pu, pc, meta, named_u, named_l = pl.pallas_call(
        functools.partial(pack_kernel, n_row, n_col, tr, tc, hb, nb, kk, kinds),
        out_shape=(jax.ShapeDtypeStruct((full_u,) + block, bf16), jax.ShapeDtypeStruct((full_l,) + block, bf16),
                   jax.ShapeDtypeStruct((3,), jnp.int32), jax.ShapeDtypeStruct(named, jnp.float32),
                   jax.ShapeDtypeStruct(named, jnp.float32)),
        in_specs=[smem, smem, hbm, hbm], out_specs=(hbm, hbm, smem, vmem, vmem),
        scratch_shapes=[pltpu.SMEM((n_ku * (2 * hb + 1),), jnp.int32), pltpu.SMEM((n_kl * (nb + 1),), jnp.int32),
                        pltpu.VMEM((full_u,) + block, bf16), pltpu.VMEM((full_l,) + block, bf16), dma, dma],
        compiler_params=pltpu.CompilerParams(vmem_limit_bytes=60 * 2**20),
        name="pack",
    )(cols_list.reshape(-1), rows_list.reshape(-1), row_panels, col_panels)

    n_all = n_row * 2 * full_u + 4 * carry_max
    tab_rows = 2 * (1 + sw) * 2 * LEAFROWS

    def exchange(which):
        def run(meta, named_u, named_l, pu, pc, separator, inverses):
            g, gc, tab, acc = pl.pallas_call(
                functools.partial(comm_kernel, n_row, n_col, tr, tc, hb, nb, full_u, full_l, carry_max, kinds[which]),
                out_shape=(jax.ShapeDtypeStruct((n_all,) + block, bf16),
                           jax.ShapeDtypeStruct((2 * n_col * full_l,) + block, bf16),
                           jax.ShapeDtypeStruct((tab_rows, BLK), jnp.int32),
                           pltpu.VMEM((loc_rows + BLK, half + BLK), jnp.float32)),
                in_specs=[smem, vmem, vmem, hbm, hbm, hbm], out_specs=(hbm, hbm, vmem, vmem),
                scratch_shapes=[pltpu.VMEM((2 * over,) + block, bf16),
                                *[pltpu.VMEM((carry_max,) + block, bf16)] * 4]
                + [dma((2, n_row, PARTS))] * 4 + [dma((n_col,))] * 4 + [dma((2,))] * 7 + [dma((6,))],
                compiler_params=pltpu.CompilerParams(collective_id=which, has_side_effects=True,
                                                     vmem_limit_bytes=40 * 2**20),
                name="exchange%d" % which,
            )(meta, named_u, named_l, pu, pc, separator)
            return solve_call(n_row, n_col, hb, nb, kk, full_l)(tab, inverses, g, gc, acc)
        return run

    return lax.switch(meta[0], [exchange(i) for i in range(len(kinds))],
                      meta, named_u, named_l, pu, pc, separator, inverses)


def solution(mesh):
    placed = (
        P("row", "col"),
        P("leaf", "row", "col"),
        P("leaf", "row", "col"),
        P(),
        P(),
        P("row", None),
    )
    n_row, n_col = mesh.shape["row"], mesh.shape["col"]

    def per_device(separator, col_panels, row_panels, *rest):
        whole = separator.shape[1] % (2 * W) == 0 and separator.shape[0] % W == 0
        fits = (rest[0].shape[1] <= LEAFROWS and 3 <= n_row <= LEAFROWS and n_col <= LEAFROWS
                and n_row * separator.shape[0] <= BLK * BLK and n_col * separator.shape[1] <= BLK * BLK)
        if whole and row_panels.shape[1] % BLK == 0 and col_panels.shape[2] % BLK == 0 and mesh.shape["leaf"] == 2 and fits:
            return sparse_device(n_row, n_col, separator, col_panels, row_panels, *rest)
        return dense_device(separator, col_panels, row_panels, *rest)

    return jax.shard_map(
        per_device, mesh=mesh, in_specs=placed, out_specs=P("row", ("col", "leaf")), check_vma=False
    )
```

```python
import functools

import jax
import jax.numpy as jnp
from jax import lax
from jax.experimental import pallas as pl
from jax.experimental.pallas import tpu as pltpu
from jax.sharding import PartitionSpec as P

W = 256
BLK = 128
MESH = pl.DeviceIdType.MESH
PARTS = 2
LEAFROWS = 8


def touched(index_list, positions):
    return jnp.any(index_list[:, :, :, None] == (positions // BLK)[None, None, None, :], axis=2)


def dense_device(separator, col_panels, row_panels, rows_list, cols_list, inverses):
    loc_rows = separator.shape[0]
    loc_cols = separator.shape[1]
    half = loc_cols // 2
    mine = lax.axis_index("leaf")
    row_ids = lax.axis_index("row") * loc_rows + jnp.arange(loc_rows, dtype=jnp.int32)
    subtrees = jnp.stack([mine])
    col_ids = lax.axis_index("col") * loc_cols + jnp.arange(loc_cols, dtype=jnp.int32)
    row_mask = touched(jnp.take(rows_list, subtrees, axis=0), row_ids)
    col_mask = touched(jnp.take(cols_list, subtrees, axis=0), col_ids)
    upper_all = lax.all_gather(row_panels, "row", axis=1, tiled=True)
    owner_all = jnp.arange(upper_all.shape[1], dtype=jnp.int32) // W
    keep_upper = jnp.take(col_mask, owner_all, axis=1)
    upper_all = jnp.where(keep_upper, upper_all, jnp.zeros_like(upper_all))
    piece = lax.all_gather(col_panels, "col", axis=2, tiled=True)
    owner = jnp.arange(piece.shape[2], dtype=jnp.int32) // W
    keep_lower = jnp.transpose(jnp.take(row_mask, owner, axis=1), (0, 2, 1))
    masked = jnp.where(keep_lower, piece, jnp.zeros_like(piece))
    update = jnp.einsum("srj,sjc->rc", masked, upper_all, preferred_element_type=jnp.float32)
    own_part = lax.dynamic_slice_in_dim(separator, mine * half, half, 1)
    both = lax.psum_scatter(update, "leaf", scatter_dimension=1, tiled=True)
    combined = own_part - both
    blocks = combined.reshape(loc_rows // W, W, half)
    factor = inverses.reshape(loc_rows // W, W, W)
    solved = jnp.einsum("bij,bjc->bic", factor, blocks, precision=lax.Precision.HIGHEST)
    return solved.reshape(loc_rows, half)


def mm(a, b):
    return jnp.dot(a.astype(jnp.bfloat16), b.astype(jnp.bfloat16), preferred_element_type=jnp.float32)


def grid_ids(shape):
    return lax.broadcasted_iota(jnp.int32, shape, 0), lax.broadcasted_iota(jnp.int32, shape, 1)


def ones_where(mask):
    return jnp.where(mask, jnp.float32(1), jnp.float32(0))


def list_mask(lists, leaves, kk, held):
    width = lists.shape[0] // (leaves * kk)
    lane = lax.broadcasted_iota(jnp.int32, (1, BLK), 1)
    held[...] = jnp.zeros(held.shape, jnp.float32)
    for leaf in range(leaves):
        for k in range(kk):
            at = (leaf * kk + k) * width
            hit = lane == lists[at]
            for e in range(1, width):
                hit = jnp.logical_or(hit, lane == lists[at + e])
            held[leaf * LEAFROWS + k:leaf * LEAFROWS + k + 1, :] = ones_where(hit)
    return held[...]


def slice_counts(tr, sw, n_own):
    y, m = grid_ids((2 * LEAFROWS, 2 * LEAFROWS))
    same = jnp.logical_and(y // LEAFROWS == m // LEAFROWS, y % LEAFROWS < n_own)
    total = jnp.zeros(y.shape, jnp.float32)
    for t in range(tr):
        s = (y % LEAFROWS) * tr + t
        first = (m % LEAFROWS) * sw
        total = total + ones_where(same & (s >= first) & (s < first + sw))
    return total


def core_tails(counts, base):
    y, m = grid_ids((2 * LEAFROWS, 2 * LEAFROWS))
    past = jnp.maximum(counts - base, 0.0)
    chip = mm(ones_where(y % LEAFROWS == m % LEAFROWS), past)
    core = lax.broadcasted_iota(jnp.int32, past.shape, 0) // LEAFROWS
    carried = jnp.floor((chip + 1.0 - core.astype(jnp.float32)) * 0.5)
    return past, carried


def pack_kernel(n_row, n_col, tr, tc, hb, nb, kk, kinds, cols_s, rows_s, upper, lower,
                pu, pc, meta, named_u, named_l, flag_u, flag_l, pu_v, pc_v, sem_in, sem_out):
    r, c, mine = lax.axis_index("row"), lax.axis_index("col"), lax.axis_index("leaf")
    sw = W // BLK
    wb = 2 * hb
    n_ku, n_kl = -(-tr // sw) + 1, -(-tc // sw) + 1
    width_u, width_l = cols_s.shape[0] // (2 * kk), rows_s.shape[0] // (2 * kk)
    first_u, first_l = r * tr // sw, c * tc // sw

    @pl.loop(0, n_ku * (wb + 1))
    def _(i):
        flag_u[i] = jnp.int32(0)

    @pl.loop(0, n_kl * (nb + 1))
    def _(i):
        flag_l[i] = jnp.int32(0)

    for q in range(n_ku):
        at = (mine * kk + jnp.minimum(first_u + q, kk - 1)) * width_u
        for e in range(width_u):
            v = cols_s[at + e] - c * wb
            flag_u[q * (wb + 1) + jnp.where((v >= 0) & (v < wb), v, wb)] = jnp.int32(1)
    for q in range(n_kl):
        at = (mine * kk + jnp.minimum(first_l + q, kk - 1)) * width_l
        for e in range(width_l):
            v = rows_s[at + e] - r * nb
            flag_l[q * (nb + 1) + jnp.where((v >= 0) & (v < nb), v, nb)] = jnp.int32(1)

    n_u = n_l = jnp.int32(0)
    for t in range(tr):
        flags = ((r * tr + t) // sw - first_u) * (wb + 1)

        def take_upper(j, n, t=t, flags=flags):
            hit = flag_u[flags + j]

            @pl.when(hit > 0)
            def _():
                src = upper.at[0, pl.ds(t * BLK, BLK), pl.ds(pl.multiple_of(j * BLK, BLK), BLK)]
                pltpu.make_async_copy(src, pu_v.at[n], sem_in).start()
            return n + hit

        n_u = lax.fori_loop(0, wb, take_upper, n_u)
    for t in range(tc):
        flags = ((c * tc + t) // sw - first_l) * (nb + 1)

        def take_lower(j, n, t=t, flags=flags):
            hit = flag_l[flags + j]

            @pl.when(hit > 0)
            def _():
                src = lower.at[0, pl.ds(pl.multiple_of(j * BLK, BLK), BLK), pl.ds(t * BLK, BLK)]
                pltpu.make_async_copy(src, pc_v.at[n], sem_in).start()
            return n + hit

        n_l = lax.fori_loop(0, nb, take_lower, n_l)

    row, lane = grid_ids((2 * LEAFROWS, BLK))
    J, x = grid_ids((BLK, BLK))
    cnt = mm(list_mask(cols_s, 2, kk, named_u), ones_where((J >= x * wb) & (J < (x + 1) * wb)))
    counts = mm(slice_counts(tr, sw, n_row), cnt)
    cnt_l = mm(list_mask(rows_s, 2, kk, named_l), ones_where((J >= x * nb) & (J < (x + 1) * nb)))
    counts_l = mm(slice_counts(tc, sw, n_col), cnt_l)
    base = kinds[0][0]
    past, carried = core_tails(counts, base)
    y, m = grid_ids((2 * LEAFROWS, 2 * LEAFROWS))
    same = y // LEAFROWS == m // LEAFROWS
    hop, src = y % LEAFROWS, m % LEAFROWS
    live = same & (hop <= n_row - 2) & (src < n_row)
    most = jnp.maximum(mm(ones_where(live & (src <= hop)), carried),
                       mm(ones_where(live & (src >= n_row - 1 - hop)), carried))
    hops = [jnp.max(jnp.where(row % LEAFROWS == h, most, 0.0)).astype(jnp.int32) for h in range(n_row - 1)]
    most_past = jnp.max(past).astype(jnp.int32)
    most_u = jnp.max(counts).astype(jnp.int32)
    most_l = jnp.max(counts_l).astype(jnp.int32)
    level = jnp.int32(0)
    for cap, over, carry, cap_l in kinds[:-1]:
        bad = most_l > cap_l
        if over:
            bad = jnp.logical_or(bad, most_past > over)
            for h in range(n_row - 1):
                bad = jnp.logical_or(bad, hops[h] > carry[h])
        else:
            bad = jnp.logical_or(bad, most_u > cap)
        level = level + bad.astype(jnp.int32)
    meta[0] = level
    for leaf in range(2):
        meta[1 + leaf] = jnp.sum(jnp.where((row == leaf * LEAFROWS + r) & (lane == c), past, 0.0)).astype(jnp.int32)

    @pl.loop(0, n_u + n_l)
    def _(i):
        pltpu.make_async_copy(pu.at[0], pu_v.at[0], sem_in).wait()

    step = 8

    def put(i, full, src, dst):
        at = pl.ds(jnp.minimum(i * step, full - step), step)
        return pltpu.make_async_copy(src.at[at], dst.at[at], sem_out)

    @pl.loop(0, (n_u + step - 1) // step)
    def _(i):
        put(i, pu.shape[0], pu_v, pu).start()

    @pl.loop(0, (n_l + step - 1) // step)
    def _(i):
        put(i, pc.shape[0], pc_v, pc).start()

    @pl.loop(0, (n_u + step - 1) // step + (n_l + step - 1) // step)
    def _(i):
        put(0, pu.shape[0], pu_v, pu).wait()


def gather_tables(n_row, n_col, tr, tc, hb, nb, base, full_u, full_l, carry_max, named_u, named_l, tab):
    r, c, mine = lax.axis_index("row"), lax.axis_index("col"), lax.axis_index("leaf")
    sw, wb = W // BLK, 2 * hb
    rows = 2 * LEAFROWS
    row, lane = grid_ids((rows, BLK))
    J, x = grid_ids((BLK, BLK))
    y, m = grid_ids((rows, rows))
    leaf, k = row // LEAFROWS, row % LEAFROWS
    before = ones_where(J < x)
    every = jnp.ones((BLK, BLK), jnp.float32)

    def pick(start, count):
        return ones_where((J == start + x) & (x < count))

    def slices(q, per, n_own):
        s = k * sw + q
        owner = jnp.zeros(s.shape, jnp.int32)
        for o in range(1, n_own):
            owner = owner + (s >= o * per).astype(jnp.int32)
        s_y = (y % LEAFROWS) * sw + q
        own_y = jnp.zeros(y.shape, jnp.int32)
        for o in range(1, n_own):
            own_y = own_y + (s_y >= o * per).astype(jnp.int32)
        weight = jnp.zeros(y.shape, jnp.float32)
        for other in range(sw):
            s_m = (m % LEAFROWS) * sw + other
            weight = weight + ones_where((y // LEAFROWS == m // LEAFROWS) & (s_m >= own_y * per) & (s_m < s_y))
        return owner, own_y, weight

    def store(mask, locs, n, at):
        rank = mm(mask, before)
        count = mm(mask, every)
        outs = [jnp.full(mask.shape, float(n), jnp.float32)] + [jnp.zeros(mask.shape, jnp.float32) for _ in locs]
        for i in range(n):
            sel = (mask > 0) & (rank == float(i))
            vals = [lane.astype(jnp.float32)] + locs
            for o in range(len(outs)):
                got = jnp.sum(jnp.where(sel, vals[o], 0.0), axis=1, keepdims=True)
                outs[o] = jnp.where((lane == i) & (count > float(i)), got, outs[o])
        outs[0] = jnp.where(lane == BLK // 2, count, outs[0])
        for o, v in enumerate(outs):
            tab[(at + o) * rows:(at + o + 1) * rows, :] = v.astype(jnp.int32)

    mask = named_u[...]
    chip = mm(mask, pick(c * wb, wb))
    cnt = mm(chip, every)
    rank = mm(chip, before)
    past, carried = core_tails(mm(slice_counts(tr, sw, n_row), cnt), base)
    half = pick(mine * hb, hb)
    mask_h, rank_h = mm(chip, half), mm(rank, half)
    locs = []
    for q in range(sw):
        owner, own_y, weight = slices(q, tr, n_row)
        p = mm(weight, cnt) + rank_h
        mine_y = m % LEAFROWS
        added = mm(ones_where((y // LEAFROWS == 1) & (m // LEAFROWS == 0) & (mine_y == own_y)), past)
        inner = ((own_y < mine_y) & (mine_y < r)) | ((r < mine_y) & (mine_y < own_y))
        passed = [mm(ones_where((m // LEAFROWS == a) & inner & (mine_y < n_row)), carried) for a in range(2)]
        e = p - base + added
        e_half = jnp.floor(e * 0.5)
        odd = e - 2.0 * e_half > 0.5
        plain = (owner * 2 + leaf).astype(jnp.float32) * full_u + p
        region = jnp.where(owner < r, n_row * 2 * full_u, n_row * 2 * full_u + 2 * carry_max).astype(jnp.float32)
        far = region + e_half + jnp.where(odd, passed[1] + carry_max, passed[0])
        locs.append(jnp.where((p < base) | (owner == r), plain, far))
    store(mask_h, locs, hb, 0)

    mask = named_l[...]
    mine_l = mm(mask, pick(r * nb, nb))
    cnt = mm(mine_l, every)
    rank = mm(mine_l, before)
    locs = []
    for q in range(sw):
        owner, _, weight = slices(q, tc, n_col)
        locs.append((leaf * n_col + owner).astype(jnp.float32) * full_l + mm(weight, cnt) + rank)
    store(mine_l, locs, nb, 1 + sw)


def comm_kernel(n_row, n_col, tr, tc, hb, nb, full_u, full_l, carry_max, kind,
                meta, named_u, named_l, pu, pc, sep, g, gc, tab, acc,
                tl, mv0, mv1, mo0, mo1, su, ru, sb, rb, sl, rl, sf, rf, sm, rm, sd, rd, so, st, rt, lo):
    base, over, carry, cap_l = kind
    mv, mo = (mv0, mv1), (mo0, mo1)
    r, c, mine = lax.axis_index("row"), lax.axis_index("col"), lax.axis_index("leaf")
    nl = pl.ds(0, cap_l)

    def low_slot(slot):
        return pl.ds(slot * full_l, cap_l)

    barrier = pltpu.get_barrier_semaphore()
    for d in (1, n_row - 1):
        pl.semaphore_signal(barrier, inc=1, device_id={"row": lax.rem(r + d, n_row)}, device_id_type=MESH)
    for d in range(1, n_col):
        pl.semaphore_signal(barrier, inc=1, device_id={"col": lax.rem(c + d, n_col)}, device_id_type=MESH)
    pl.semaphore_signal(barrier, inc=1, device_id={"leaf": 1 - mine}, device_id_type=MESH)
    pl.semaphore_wait(barrier, n_col + 2)

    cuts = [base * x // PARTS for x in range(PARTS + 1)]
    own_at = (r * 2 + mine) * full_u
    pair_id = {"leaf": 1 - mine}

    def blocks(shard, part, leaf):
        return g.at[pl.ds((shard * 2 + leaf) * full_u + cuts[part], cuts[part + 1] - cuts[part])]

    def line(way, step, part, shard, target):
        src = pu.at[pl.ds(cuts[part], cuts[part + 1] - cuts[part])] if step == 0 else blocks(shard, part, mine)
        return pltpu.make_async_remote_copy(
            src_ref=src, dst_ref=blocks(shard, part, mine), send_sem=su.at[way, step, part],
            recv_sem=ru.at[way, step, part], device_id={"row": target}, device_id_type=MESH)

    def line_send(way, step, part, act):
        goes = jnp.logical_and(r >= 1, r + step <= n_row - 1) if way == 0 else jnp.logical_and(r <= n_row - 2, r >= step)

        @pl.when(goes)
        def _():
            act(line(way, step, part, r + step if way == 0 else r - step, r - 1 if way == 0 else r + 1))

    def came(way, step):
        return r + 1 + step <= n_row - 1 if way == 0 else r >= 1 + step

    def shard_of(way, step):
        return r + 1 + step if way == 0 else r - 1 - step

    def line_wait(way, step, part):
        @pl.when(came(way, step))
        def _():
            line(way, step, part, shard_of(way, step), r + 1 if way == 0 else r - 1).wait_recv()

    def hand(way, step, part, leaf):
        at = blocks(shard_of(way, step), part, leaf)
        return pltpu.make_async_remote_copy(
            src_ref=at, dst_ref=at, send_sem=sb.at[way, step, part], recv_sem=rb.at[way, step, part],
            device_id=pair_id, device_id_type=MESH)

    def hand_if(way, step, part, leaf, act):
        @pl.when(came(way, step))
        def _():
            act(hand(way, step, part, leaf))

    def hand_own(leaf):
        at = g.at[pl.ds((r * 2 + leaf) * full_u, base + over)]
        return pltpu.make_async_remote_copy(
            src_ref=pu.at[pl.ds(0, base + over)] if leaf is mine else at, dst_ref=at, send_sem=so.at[0],
            recv_sem=so.at[1], device_id=pair_id, device_id_type=MESH)

    def across(d, slot):
        return pltpu.make_async_remote_copy(
            src_ref=pc.at[nl], dst_ref=gc.at[low_slot(slot)], send_sem=sl.at[d], recv_sem=rl.at[d],
            device_id={"col": lax.rem(c + d, n_col)}, device_id_type=MESH)

    def from_slot(d, leaf):
        return leaf * n_col + lax.rem(c + n_col - d, n_col)

    def pair(d, leaf):
        slot = from_slot(d, leaf)
        return pltpu.make_async_remote_copy(
            src_ref=pc.at[nl] if d == 0 else gc.at[low_slot(slot)], dst_ref=gc.at[low_slot(slot)],
            send_sem=sf.at[d], recv_sem=rf.at[d], device_id=pair_id, device_id_type=MESH)

    def tail(leaf):
        return pltpu.make_async_remote_copy(
            src_ref=pu.at[pl.ds(base, over)], dst_ref=tl.at[pl.ds(leaf * over, over)], send_sem=st.at[0],
            recv_sem=st.at[1], device_id=pair_id, device_id_type=MESH)

    tail_here = pltpu.make_async_copy(pu.at[pl.ds(base, over)], tl.at[pl.ds(mine * over, over)], lo.at[2]) if over else None
    own_here = pltpu.make_async_copy(pu.at[pl.ds(0, base + over)], g.at[pl.ds(own_at, base + over)], lo.at[0])
    half = hb * BLK
    fill = pltpu.make_async_copy(
        sep.at[:, pl.ds(pl.multiple_of(mine * half, half), half)],
        acc.at[pl.ds(0, nb * BLK), pl.ds(0, half)], lo.at[5])
    low_here = pltpu.make_async_copy(pc.at[nl], gc.at[low_slot(mine * n_col + c)], lo.at[1])

    def carry_copy(way, h, target):
        n = pl.ds(0, carry[h])
        return pltpu.make_async_remote_copy(
            src_ref=mo[way].at[n], dst_ref=mv[way].at[n], send_sem=sm.at[way], recv_sem=rm.at[way],
            device_id={"row": target}, device_id_type=MESH)

    def carry_at(way, h, leaf):
        start = n_row * 2 * full_u + (2 * carry_max if way == 0 else 0) + leaf * carry_max
        return g.at[pl.ds(start, carry[h])]

    def carry_hand(way, h, leaf):
        at = carry_at(way, h, leaf)
        return pltpu.make_async_remote_copy(
            src_ref=mv[way].at[pl.ds(0, carry[h])] if leaf is mine else at, dst_ref=at, send_sem=sd.at[way],
            recv_sem=rd.at[way], device_id=pair_id, device_id_type=MESH)

    def carry_here(way, h):
        return pltpu.make_async_copy(mv[way].at[pl.ds(0, carry[h])], carry_at(way, h, mine), lo.at[3 + way])

    def next_row(way):
        return r - 1 if way == 0 else r + 1

    def merge(way, h):
        t0, t1 = meta[1], meta[2]
        n_here = (t0 + t1 + 1 - mine) // 2

        @pl.loop(0, carry[h])
        def _(i):
            e = 2 * i + mine
            own = tl[jnp.clip(jnp.where(e < t0, e, over + e - t0), 0, 2 * over - 1)]
            if h > 0:
                prev = mv[way][jnp.clip(i - n_here, 0, carry[h - 1] - 1)]
                own = jnp.where(i < n_here, own, prev)
            mo[way][i] = own

    def at_hop(way, h):
        return n_row - 1 - h if way == 0 else h

    if over:
        tail(mine).start()
        tail_here.start()
    for part in range(PARTS):
        for way in range(2):
            line_send(way, 0, part, lambda copy: copy.start())
    for d in range(1, n_col):
        across(d, mine * n_col + c).start()
    pair(0, mine).start()
    hand_own(mine).start()
    own_here.start()
    fill.start()
    low_here.start()
    if over:
        tail(1 - mine).wait_recv()
        tail_here.wait()
        for way in range(2):
            @pl.when(r == at_hop(way, 0))
            def _(way=way):
                merge(way, 0)
                carry_copy(way, 0, next_row(way)).start()
    gather_tables(n_row, n_col, tr, tc, hb, nb, base, full_u, full_l, carry_max, named_u, named_l, tab)
    for step in range(n_row - 1):
        for part in range(PARTS):
            for way in range(2):
                line_wait(way, step, part)
                if step < n_row - 2:
                    line_send(way, step + 1, part, lambda copy: copy.start())
                hand_if(way, step, part, mine, lambda copy: copy.start())
        if over:
            for way in range(2):
                @pl.when(r == at_hop(way, step + 1))
                def _(way=way):
                    carry_copy(way, step, next_row(1 - way)).wait_recv()
                    if step < n_row - 2:
                        merge(way, step + 1)
                    carry_hand(way, step, mine).start()
                    carry_here(way, step).start()
                    if step < n_row - 2:
                        carry_copy(way, step + 1, next_row(way)).start()
        if step == 1:
            for d in range(1, n_col):
                across(d, from_slot(d, mine)).wait_recv()
                pair(d, mine).start()
    for d in range(n_col):
        pair(d, 1 - mine).wait_recv()
    hand_own(1 - mine).wait_recv()
    for step in range(n_row - 1):
        for part in range(PARTS):
            for way in range(2):
                hand_if(way, step, part, 1 - mine, lambda copy: copy.wait_recv())
    if over:
        for step in range(n_row - 1):
            for way in range(2):
                @pl.when(r == at_hop(way, step + 1))
                def _(way=way):
                    carry_hand(way, step, 1 - mine).wait_recv()
                    carry_hand(way, step, mine).wait_send()
                    carry_here(way, step).wait()

                @pl.when(r == at_hop(way, step))
                def _(way=way):
                    carry_copy(way, step, next_row(way)).wait_send()
        tail(mine).wait_send()
    own_here.wait()
    fill.wait()
    low_here.wait()
    hand_own(mine).wait_send()
    for d in range(n_col):
        pair(d, mine).wait_send()
    for d in range(1, n_col):
        across(d, mine * n_col + c).wait_send()
    for step in range(n_row - 1):
        for part in range(PARTS):
            for way in range(2):
                line_send(way, step, part, lambda copy: copy.wait_send())
                hand_if(way, step, part, mine, lambda copy: copy.wait_send())


def split(x):
    hi = x.astype(jnp.bfloat16)
    return hi, (x - hi.astype(jnp.float32)).astype(jnp.bfloat16)


GROUP = 4


def solve_kernel(n_row, n_col, hb, nb, kk, full_l, tab, inv, g, gc, acc, out, _, low, up, stage, sem, out_sem):
    sw = W // BLK
    half, loc_rows = hb * BLK, nb * BLK
    rows_of = 2 * LEAFROWS
    row_tab = (1 + sw) * rows_of

    def row_of(m):
        return m // kk * LEAFROWS + lax.rem(m, kk)

    @pl.loop(0, 2 * kk)
    def _(m):
        at_m = row_of(m)

        @pl.loop(0, tab[at_m, BLK // 2])
        def _(n):
            at = pl.ds(pl.multiple_of(n * BLK, BLK), BLK)
            for q in range(sw):
                src = g.at[tab[(1 + q) * rows_of + at_m, n]]
                pltpu.make_async_copy(src, up.at[m, pl.ds(q * BLK, BLK), at], sem.at[m]).start()

        @pl.loop(0, tab[row_tab + at_m, BLK // 2])
        def _(n):
            at = pl.ds(pl.multiple_of(n * BLK, BLK), BLK)
            for q in range(sw):
                src = gc.at[tab[row_tab + (1 + q) * rows_of + at_m, n]]
                pltpu.make_async_copy(src, low.at[m, at, pl.ds(q * BLK, BLK)], sem.at[m]).start()

    wide = GROUP * BLK

    @pl.loop(0, 2 * kk)
    def _(m):
        at_m = row_of(m)
        n_u, n_l = tab[at_m, BLK // 2], tab[row_tab + at_m, BLK // 2]

        @pl.loop(0, (n_u + n_l) * sw)
        def _(n):
            pltpu.make_async_copy(g.at[0], low.at[m, pl.ds(0, BLK), pl.ds(0, BLK)], sem.at[m]).wait()

        def subtract(first, count):
            rows = pl.ds(pl.multiple_of(first * BLK, BLK), count * BLK)

            @pl.loop(0, (n_u + GROUP - 1) // GROUP)
            def _(y):
                cols = pl.ds(pl.multiple_of(y * wide, wide), wide)
                prod = jnp.dot(low[m, rows, :], up[m, :, cols], preferred_element_type=jnp.float32)
                for i in range(count):
                    row = tab[row_tab + at_m, first + i]
                    to = pl.ds(pl.multiple_of(row * BLK, BLK), BLK)
                    for j in range(GROUP):
                        col = tab[at_m, y * GROUP + j]
                        at = pl.ds(pl.multiple_of(col * BLK, BLK), BLK)
                        acc[to, at] -= prod[i * BLK:(i + 1) * BLK, j * BLK:(j + 1) * BLK]

        short = GROUP // 2
        whole = (n_l + GROUP - 1 - short) // GROUP

        @pl.loop(0, whole)
        def _(x):
            subtract(x * GROUP, GROUP)

        @pl.when(n_l > whole * GROUP)
        def _():
            subtract(whole * GROUP, short)

    tile = min(512, half)
    steps = loc_rows // W

    def put(b, slot):
        return pltpu.make_async_copy(stage.at[slot], out.at[pl.ds(pl.multiple_of(b * W, W), W)], out_sem.at[slot])

    @pl.loop(0, steps)
    def _(b):
        slot = lax.rem(b, 2)

        @pl.when(b >= 2)
        def _():
            put(b - 2, slot).wait()

        rows = pl.ds(pl.multiple_of(b * W, W), W)
        f_hi, f_lo = split(inv[rows, :])
        for n in range(half // tile):
            at = pl.ds(n * tile, tile)
            hi, lo = split(acc[rows, at])
            stage[slot, :, at] = (jnp.dot(f_hi, hi, preferred_element_type=jnp.float32)
                                  + (jnp.dot(f_hi, lo, preferred_element_type=jnp.float32)
                                     + jnp.dot(f_lo, hi, preferred_element_type=jnp.float32)))
        put(b, slot).start()

    for b in range(max(0, steps - 2), steps):
        put(b, b % 2).wait()


def solve_call(n_row, n_col, hb, nb, kk, full_l):
    hbm = pl.BlockSpec(memory_space=pl.ANY)
    half, loc_rows = hb * BLK, nb * BLK
    hg, ng = -(-hb // GROUP) * GROUP, -(-nb // GROUP) * GROUP
    vmem = pl.BlockSpec(memory_space=pltpu.VMEM)
    acc = pltpu.VMEM((loc_rows + BLK, half + BLK), jnp.float32)

    def run(tab, *args):
        return pl.pallas_call(
            functools.partial(solve_kernel, n_row, n_col, hb, nb, kk, full_l),
            out_shape=(jax.ShapeDtypeStruct((loc_rows, half), jnp.float32), acc),
            in_specs=[pl.BlockSpec(memory_space=pltpu.SMEM), vmem, hbm, hbm, vmem], out_specs=(hbm, vmem),
            scratch_shapes=[pltpu.VMEM((2 * kk, ng * BLK, W), jnp.bfloat16),
                            pltpu.VMEM((2 * kk, W, hg * BLK), jnp.bfloat16),
                            pltpu.VMEM((2, W, half), jnp.float32),
                            pltpu.SemaphoreType.DMA((2 * kk,)), pltpu.SemaphoreType.DMA((2,))],
            input_output_aliases={4: 1},
            compiler_params=pltpu.CompilerParams(vmem_limit_bytes=40 * 2**20),
            name="solve",
        )(tab, *args)[0]
    return run


def kinds_of(full_u, full_l, n_row):
    base, over = -(-full_u * 20 // 96), -(-full_u * 24 // 96)
    found = []
    for last, inner, first, low in ((12, 12, 12, 22), (14, 14, 14, 24), (15, 15, 14, 24), (16, 16, 14, 24), (17, 16, 14, 24),
                                    (19, 17, 15, 26), (22, 19, 16, 26), (32, 28, 20, 28)):
        sizes = [first] + [inner] * (n_row - 3) + [last]
        found.append((base, over, tuple(-(-full_u * v // 96) for v in sizes[:n_row - 1]), -(-full_l * low // 48)))
    found.append((-(-full_u * 48 // 96), 0, None, -(-full_l * 40 // 48)))
    found.append((full_u, 0, None, full_l))
    return found


def sparse_device(n_row, n_col, separator, col_panels, row_panels, rows_list, cols_list, inverses):
    loc_rows, loc_cols = separator.shape
    half = loc_cols // 2
    tr, tc = row_panels.shape[1] // BLK, col_panels.shape[2] // BLK
    hb, nb = half // BLK, loc_rows // BLK
    kk = rows_list.shape[1]
    sw = W // BLK
    full_u, full_l = 2 * tr * hb, tc * nb
    kinds = kinds_of(full_u, full_l, n_row)
    carry_max = max(max(kind[2]) for kind in kinds if kind[2])
    over = kinds[0][1]

    block = (BLK, BLK)
    bf16 = jnp.bfloat16
    hbm = pl.BlockSpec(memory_space=pl.ANY)
    vmem = pl.BlockSpec(memory_space=pltpu.VMEM)
    smem = pl.BlockSpec(memory_space=pltpu.SMEM)
    dma = pltpu.SemaphoreType.DMA
    n_ku, n_kl = -(-tr // sw) + 1, -(-tc // sw) + 1
    named = (2 * LEAFROWS, BLK)
    pu, pc, meta, named_u, named_l = pl.pallas_call(
        functools.partial(pack_kernel, n_row, n_col, tr, tc, hb, nb, kk, kinds),
        out_shape=(jax.ShapeDtypeStruct((full_u,) + block, bf16), jax.ShapeDtypeStruct((full_l,) + block, bf16),
                   jax.ShapeDtypeStruct((3,), jnp.int32), jax.ShapeDtypeStruct(named, jnp.float32),
                   jax.ShapeDtypeStruct(named, jnp.float32)),
        in_specs=[smem, smem, hbm, hbm], out_specs=(hbm, hbm, smem, vmem, vmem),
        scratch_shapes=[pltpu.SMEM((n_ku * (2 * hb + 1),), jnp.int32), pltpu.SMEM((n_kl * (nb + 1),), jnp.int32),
                        pltpu.VMEM((full_u,) + block, bf16), pltpu.VMEM((full_l,) + block, bf16), dma, dma],
        compiler_params=pltpu.CompilerParams(vmem_limit_bytes=60 * 2**20),
        name="pack",
    )(cols_list.reshape(-1), rows_list.reshape(-1), row_panels, col_panels)

    n_all = n_row * 2 * full_u + 4 * carry_max
    tab_rows = 2 * (1 + sw) * 2 * LEAFROWS

    def exchange(which):
        def run(meta, named_u, named_l, pu, pc, separator, inverses):
            g, gc, tab, acc = pl.pallas_call(
                functools.partial(comm_kernel, n_row, n_col, tr, tc, hb, nb, full_u, full_l, carry_max, kinds[which]),
                out_shape=(jax.ShapeDtypeStruct((n_all,) + block, bf16),
                           jax.ShapeDtypeStruct((2 * n_col * full_l,) + block, bf16),
                           jax.ShapeDtypeStruct((tab_rows, BLK), jnp.int32),
                           pltpu.VMEM((loc_rows + BLK, half + BLK), jnp.float32)),
                in_specs=[smem, vmem, vmem, hbm, hbm, hbm], out_specs=(hbm, hbm, vmem, vmem),
                scratch_shapes=[pltpu.VMEM((2 * over,) + block, bf16),
                                *[pltpu.VMEM((carry_max,) + block, bf16)] * 4]
                + [dma((2, n_row, PARTS))] * 4 + [dma((n_col,))] * 4 + [dma((2,))] * 7 + [dma((6,))],
                compiler_params=pltpu.CompilerParams(collective_id=which, has_side_effects=True,
                                                     vmem_limit_bytes=40 * 2**20),
                name="exchange%d" % which,
            )(meta, named_u, named_l, pu, pc, separator)
            return solve_call(n_row, n_col, hb, nb, kk, full_l)(tab, inverses, g, gc, acc)
        return run

    return lax.switch(meta[0], [exchange(i) for i in range(len(kinds))],
                      meta, named_u, named_l, pu, pc, separator, inverses)


def solution(mesh):
    placed = (
        P("row", "col"),
        P("leaf", "row", "col"),
        P("leaf", "row", "col"),
        P(),
        P(),
        P("row", None),
    )
    n_row, n_col = mesh.shape["row"], mesh.shape["col"]

    def per_device(separator, col_panels, row_panels, *rest):
        whole = separator.shape[1] % (2 * W) == 0 and separator.shape[0] % W == 0
        fits = (rest[0].shape[1] <= LEAFROWS and 3 <= n_row <= LEAFROWS and n_col <= LEAFROWS
                and n_row * separator.shape[0] <= BLK * BLK and n_col * separator.shape[1] <= BLK * BLK)
        if whole and row_panels.shape[1] % BLK == 0 and col_panels.shape[2] % BLK == 0 and mesh.shape["leaf"] == 2 and fits:
            return sparse_device(n_row, n_col, separator, col_panels, row_panels, *rest)
        return dense_device(separator, col_panels, row_panels, *rest)

    return jax.shard_map(
        per_device, mesh=mesh, in_specs=placed, out_specs=P("row", ("col", "leaf")), check_vma=False
    )
```
